32 devices in a mesh: ctx: 4 (over z), dp: 4 (over x, core), adv: 2 (over y).
Axes of the slice: x: 2, y: 2, z: 4, core: 2. Of those that a mesh axis runs over, the one named last changes fastest.
Arguments:
- hidden: bfloat16 [2, 4, 512, 4096], P('adv', 'dp', 'ctx'), may hold values from -6 to 6
- queries: bfloat16 [2, 4, 512, 4096], P('adv', 'dp', 'ctx'), may hold values from -48 to 48
- keys: bfloat16 [2, 4, 512, 1024], P('adv', 'dp', 'ctx'), may hold values from -4.5 to 4.5
- targets: bfloat16 [2, 4, 512, 4096], P('adv', 'dp', None, 'ctx'), may hold values from -6 to 6
- lengths: int32 [2, 4, 8], P('adv', 'dp'), may hold values from 1 to 128, 512 in all within a row
- value_matrix: bfloat16 [4096, 1024], replicated, may hold values from -0.09375 to 0.09375
- attacker_down_factor: bfloat16 [4096, 16], replicated, may hold values from -0.09375 to 0.09375
- attacker_up_factor: bfloat16 [16, 1024], replicated, may hold values from -1.5 to 1.5
Outputs:
- outer_grad: float32 [4096, 1024], P('ctx', 'dp')
The draws below stay inside these ranges and needn't reach their ends.
Inputs may be any that keep to these rules, and one draw needn't show every extreme that they name: The 8 lengths of a sequence sum to 512, and the longest is exactly a quarter of 512.
All inputs are finite; a program needn't handle non-finite values.
Results may differ from the reference program's by a relative error of at most 0.008.
Values may be sent and summed in bfloat16 or wider, within the bound.
No kernel may reach another device: no remote copies, remote signals or barrier semaphores. Data moves between devices by JAX's collectives and lax.ppermute only.
A program may use at most 128 MiB of HBM per device.

```python
import math
import jax
import jax.numpy as jnp
import numpy as np
from jax import lax

MODEL_WIDTH = 4096
HEADS = 32
KV_HEADS = 8
HD = 128
ADVERSARY_RANK = 16
DOCS = 8
VALUE_WIDTH = 1024
GROUP = 4
SEQ = 512
BATCH = 4
ADVS = 2


def pair_fields(key):
    starting_value = jax.random.fold_in(key, 4177)
    key_q, key_k = jax.random.split(starting_value, 2)
    keys_arr = jnp.clip(jax.random.normal(key_k, (ADVS, BATCH, SEQ, VALUE_WIDTH), jnp.float32), -4.0, 4.0)
    queries = jnp.clip(jax.random.normal(key_q, (ADVS, BATCH, SEQ, MODEL_WIDTH), jnp.float32), -4.0, 4.0)
    return (queries, keys_arr)


def draw_queries(key, part):
    return pair_fields(key)[0].astype(jnp.bfloat16)


def draw_keys(key, part):
    return pair_fields(key)[1].astype(jnp.bfloat16)


def block_scale(own_key, extent, cuts, smallest, high):
    gain, own = 1.0, jax.random.fold_in(own_key, 6)
    for dim, parts in cuts:
        heights = jnp.exp(jax.random.uniform(jax.random.fold_in(own, dim), (parts,), jnp.float32, smallest / len(cuts), high / len(cuts)))
        gain = gain * jnp.repeat(heights, extent[dim] // parts).reshape([-1 if axis == dim else 1 for axis in range(len(extent))])
    return gain


def profile(amount, total, reach, slope):
    loads = [(1 << 20) // math.isqrt(standing ** slope) + 1 for standing in range(2, amount + 1)]
    surplus, counts = total - reach - (amount - 1), [1] * (amount - 1)
    while surplus > 0:
        movable = [i for i in range(amount - 1) if counts[i] < reach]
        pool, left = sum([loads[i] for i in movable]), surplus
        for i in movable:
            addition = min(reach - counts[i], max(1, left * loads[i] // pool), surplus)
            counts[i] = counts[i] + addition
            surplus = surplus - addition
    return np.array([reach] + counts)


def ragged(stream_key, count, total, most, skew):
    if count == 2:
        one = jax.random.randint(stream_key, (), max(1, total - most), min(most, total - 1) + 1)
        return jnp.stack([one, total - one])
    sizes = jnp.asarray(profile(count, total, most, skew), jnp.int32)
    couples = (count - 1) // 2
    donor, sink = sizes[1:1 + 2 * couples:2], sizes[2:2 + 2 * couples:2]
    slack = jnp.minimum(donor - 1, most - sink)
    passed = jax.random.randint(jax.random.fold_in(stream_key, 1), (couples,), 0, 1 << 20) % (slack + 1)
    sizes = sizes.at[1:1 + 2 * couples:2].set(donor - passed).at[2:2 + 2 * couples:2].set(sink + passed)
    return sizes[jax.random.permutation(jax.random.fold_in(stream_key, 2), count)]


def scatter_about(own_key, extent, spread, most, cuts=(), held_as=jnp.bfloat16):
    gain = block_scale(own_key, extent, cuts, -0.22, 0.18) if cuts else 1.0
    result = jax.random.normal(own_key, extent, jnp.float32) * spread * gain
    return jnp.minimum(jnp.maximum(result, -most), most).astype(held_as)


def setup_inputs(seed: int = 0) -> dict:
    key_list = jax.random.split(jax.random.key(seed), 9)
    return {
        "hidden": scatter_about(key_list[0], (ADVS, BATCH, SEQ, MODEL_WIDTH), 1.0, 6.0, ((0, 2), (1, 4), (2, 4))),
        "queries": draw_queries(jax.random.fold_in(key_list[8], 71), 0),
        "keys": draw_keys(jax.random.fold_in(key_list[8], 71), 0),
        "targets": scatter_about(key_list[3], (ADVS, BATCH, SEQ, MODEL_WIDTH), 1.0, 6.0, ((0, 2), (1, 4), (3, 4))),
        "lengths": jax.vmap(lambda own: ragged(own, DOCS, SEQ, SEQ // 4, 2))(jax.random.split(key_list[4], ADVS * BATCH)).reshape((ADVS, BATCH, DOCS)).astype(jnp.int32),
        "value_matrix": scatter_about(key_list[5], (MODEL_WIDTH, VALUE_WIDTH), MODEL_WIDTH ** -0.5, 0.09375),
        "attacker_down_factor": scatter_about(key_list[6], (MODEL_WIDTH, ADVERSARY_RANK), MODEL_WIDTH ** -0.5, 0.09375),
        "attacker_up_factor": scatter_about(key_list[7], (ADVERSARY_RANK, VALUE_WIDTH), ADVERSARY_RANK ** -0.5, 1.5),
    }


def doc_ids(lengths):
    ends = jnp.cumsum(lengths)
    position = jnp.arange(SEQ, dtype=jnp.int32)
    return lax.optimization_barrier(jnp.sum((position[:, None] >= ends[None, :]).astype(jnp.int32), axis=1))

def head_grad(q_head, k_head, v_head, y_head, docs, factor):
    scores = jnp.dot(q_head, k_head.T, preferred_element_type=jnp.float32) * HD ** (-0.5)
    position = jnp.arange(SEQ, dtype=jnp.int32)
    visible = (docs[:, None] == docs[None, :]) & (position[None, :] <= position[:, None])
    scores = jnp.where(visible, scores, -1e+30)
    top = lax.optimization_barrier(jnp.max(scores, axis=1, keepdims=True))
    expo = jnp.exp(scores - top)
    probs = (expo / lax.optimization_barrier(jnp.sum(expo, axis=1, keepdims=True))).astype(jnp.bfloat16)
    attn = jnp.dot(probs, v_head, preferred_element_type=jnp.float32)
    d_attn = (factor * (attn - y_head.astype(jnp.float32))).astype(jnp.bfloat16)
    return jnp.dot(probs.T, d_attn, preferred_element_type=jnp.float32).astype(jnp.bfloat16)

def sequence_grad(q_seq, k_seq, value_rows, y_seq, docs, factor):
    q_heads = q_seq.reshape(SEQ, HEADS, HD).transpose(1, 0, 2)
    k_heads = jnp.repeat(k_seq.reshape(SEQ, KV_HEADS, HD), GROUP, axis=1).transpose(1, 0, 2)
    v_heads = jnp.repeat(value_rows.reshape(SEQ, KV_HEADS, HD), GROUP, axis=1).transpose(1, 0, 2)
    y_heads = y_seq.reshape(SEQ, HEADS, HD).transpose(1, 0, 2)

    def one_head(item):
        return head_grad(item[0], item[1], item[2], item[3], docs, factor)
    gradient_list = lax.map(one_head, (q_heads, k_heads, v_heads, y_heads))
    grouped_rows = gradient_list.reshape(KV_HEADS, GROUP, SEQ, HD).astype(jnp.float32).sum(axis=1)
    return grouped_rows.transpose(1, 0, 2).reshape(SEQ, VALUE_WIDTH).astype(jnp.bfloat16)

def reference(hidden, queries, keys, targets, lengths, value_matrix, attacker_down_factor, attacker_up_factor):
    factor = float(BATCH * SEQ) ** (-0.5)
    total = jnp.zeros((MODEL_WIDTH, VALUE_WIDTH), jnp.float32)
    for attacker_update in range(ADVS):
        docs_all = [doc_ids(lengths[attacker_update, batch_slice]) for batch_slice in range(BATCH)]
        starting_values = [jnp.dot(hidden[attacker_update, batch_slice], value_matrix, preferred_element_type=jnp.float32) for batch_slice in range(BATCH)]

        def forward_gradients(down_factor, up_factor, sign):
            input_rows, gradient_list = ([], [])
            for batch_slice in range(BATCH):
                attacker_input = jnp.dot(hidden[attacker_update, batch_slice], down_factor, preferred_element_type=jnp.float32).astype(jnp.bfloat16)
                value_rows = (starting_values[batch_slice] + jnp.dot(attacker_input, up_factor, preferred_element_type=jnp.float32)).astype(jnp.bfloat16)
                gradient_list.append(sequence_grad(queries[attacker_update, batch_slice], keys[attacker_update, batch_slice], value_rows, targets[attacker_update, batch_slice], docs_all[batch_slice], sign * factor))
                input_rows.append(attacker_input)
            return (input_rows, gradient_list)
        input_rows, gradient_list = forward_gradients(attacker_down_factor, attacker_up_factor, 1.0)
        down_gradient = jnp.zeros((MODEL_WIDTH, ADVERSARY_RANK), jnp.float32)
        up_gradient = jnp.zeros((ADVERSARY_RANK, VALUE_WIDTH), jnp.float32)
        for batch_slice in range(BATCH):
            blended_output = jnp.dot(gradient_list[batch_slice], attacker_up_factor.T, preferred_element_type=jnp.float32).astype(jnp.bfloat16)
            down_gradient = down_gradient + jnp.dot(hidden[attacker_update, batch_slice].T, blended_output, preferred_element_type=jnp.float32)
            up_gradient = up_gradient + jnp.dot(input_rows[batch_slice].T, gradient_list[batch_slice], preferred_element_type=jnp.float32)
        count = ADVERSARY_RANK * (MODEL_WIDTH + VALUE_WIDTH)
        broadcast_rows = jnp.sqrt((jnp.sum(down_gradient * down_gradient) + jnp.sum(up_gradient * up_gradient)) / count + 1e-06)
        stepped_down_factor = (attacker_down_factor.astype(jnp.float32) - 0.01 * down_gradient / broadcast_rows).astype(jnp.bfloat16)
        stepped_up_factor = (attacker_up_factor.astype(jnp.float32) - 0.01 * up_gradient / broadcast_rows).astype(jnp.bfloat16)
        input_rows, tampers = forward_gradients(stepped_down_factor, stepped_up_factor, -1.0)
        for batch_slice in range(BATCH):
            total = total + jnp.dot(hidden[attacker_update, batch_slice].T, tampers[batch_slice], preferred_element_type=jnp.float32)
    return total / ADVS
```

```python
import functools
import jax
import jax.numpy as jnp
from jax import lax
from jax.experimental import pallas as pl
from jax.experimental.pallas import tpu as pltpu
from jax.sharding import PartitionSpec as P

HD = 128
GROUP = 4


ATTACK_STEP = 0.01

BF16 = jnp.bfloat16
F32 = jnp.float32


def dot(a, b, da, db):
    return lax.dot_general(a, b, (((da,), (db,)), ((), ())), preferred_element_type=F32)


def whole(shape):
    return pl.BlockSpec(shape, lambda *_: (0,) * len(shape))


def gram_kernel(len_ref, q_ref, k_ref, y_ref, g_ref, z_ref, g_acc, z_acc, *, docs, block, reach):
    seq = k_ref.shape[0]
    scale = HD ** (-0.5)
    ends, total = [], jnp.int32(0)
    for j in range(docs):
        total = total + len_ref[j]
        ends.append(total)
    g_acc[...] = jnp.zeros_like(g_acc)
    z_acc[...] = jnp.zeros_like(z_acc)
    for i in range(seq // block):
        at, hi = i * block, (i + 1) * block
        lo = max(0, at - reach)
        heads = [slice(h * HD, (h + 1) * HD) for h in range(GROUP)]
        q = jnp.concatenate([q_ref[at:hi, h] for h in heads], axis=0)
        y = jnp.concatenate([y_ref[at:hi, h] for h in heads], axis=0)
        scores = dot(q, k_ref[lo:hi, :], 1, 1) * scale
        row = lax.broadcasted_iota(jnp.int32, (block, 1), 0) + at
        first = jnp.zeros((block, 1), jnp.int32)
        for end in ends:
            first = jnp.where(row >= end, end, first)
        col = lax.broadcasted_iota(jnp.int32, (block, hi - lo), 1) + lo
        visible = (col >= first) & (col <= row)
        scores = scores.reshape(GROUP, block, hi - lo)
        scores = jnp.where(visible[None], scores, -1e30)
        top = jnp.max(scores, axis=2, keepdims=True)
        expo = jnp.exp(scores - top)
        probs = expo * (1.0 / jnp.sum(expo, axis=2, keepdims=True))
        probs = probs.reshape(GROUP * block, hi - lo).astype(BF16)
        g_acc[lo:hi, lo:hi] += dot(probs, probs, 0, 0)
        z_acc[lo:hi, :] += dot(probs, y, 0, 0)
    g_ref[0] = g_acc[...].astype(BF16)
    z_ref[...] = z_acc[...]


def gram(lengths, qk, targets):
    seq, width = targets.shape
    groups = width // (GROUP * HD)
    span = GROUP * HD
    return pl.pallas_call(
        functools.partial(gram_kernel, docs=lengths.shape[0], block=seq // 4, reach=seq // 4),
        grid=(groups,),
        in_specs=[
            pl.BlockSpec(memory_space=pltpu.SMEM),
            pl.BlockSpec((seq, span), lambda g: (0, g)),
            pl.BlockSpec((seq, HD), lambda g: (0, groups * GROUP + g)),
            pl.BlockSpec((seq, span), lambda g: (0, g)),
        ],
        out_specs=[
            pl.BlockSpec((1, seq, seq), lambda g: (g, 0, 0)),
            pl.BlockSpec((seq, HD), lambda g: (0, g)),
        ],
        out_shape=[
            jax.ShapeDtypeStruct((groups, seq, seq), BF16),
            jax.ShapeDtypeStruct((seq, groups * HD), F32),
        ],
        scratch_shapes=[pltpu.VMEM((seq, seq), F32), pltpu.VMEM((seq, HD), F32)],
        cost_estimate=pl.CostEstimate(
            flops=600_000_000, bytes_accessed=5_000_000, transcendentals=1_100_000
        ),
        name="gram",
    )(lengths, qk, qk, targets)


def first_kernel(g_ref, z_ref, v_ref, low_ref, up_ref, grad_ref, mixed_ref, up_grad_ref, *, factor):
    for g in range(g_ref.shape[0]):
        cols = slice(g * HD, (g + 1) * HD)
        total = dot(g_ref[g], v_ref[:, cols], 1, 0) - z_ref[:, cols]
        grad_ref[:, cols] = (factor * total).astype(BF16)
    grad = grad_ref[...]
    mixed_ref[...] = dot(up_ref[...], grad, 1, 1)
    up_grad_ref[...] = dot(low_ref[...], grad, 1, 0)


def first_pass(g, z, values, low_t, up, factor):
    seq, width = values.shape
    rank = up.shape[0]
    return pl.pallas_call(
        functools.partial(first_kernel, factor=factor),
        out_shape=[
            jax.ShapeDtypeStruct((seq, width), BF16),
            jax.ShapeDtypeStruct((rank, seq), F32),
            jax.ShapeDtypeStruct((rank, width), F32),
        ],
        cost_estimate=pl.CostEstimate(
            flops=150_000_000, bytes_accessed=2_000_000, transcendentals=0
        ),
        name="first_pass",
    )(g, z, values, low_t, up)


def second_kernel(g_ref, grad_ref, low_ref, new_low_ref, up_ref, new_up_ref, out_ref, *, factor):
    delta = dot(new_low_ref[...], new_up_ref[...], 0, 0) - dot(low_ref[...], up_ref[...], 0, 0)
    delta = delta.astype(BF16)
    for g in range(g_ref.shape[0]):
        cols = slice(g * HD, (g + 1) * HD)
        moved = factor * dot(g_ref[g], delta[:, cols], 1, 0)
        out_ref[:, cols] = (-(grad_ref[:, cols].astype(F32) + moved)).astype(BF16)


def second_pass(g, grad, low_t, new_low_t, up, new_up, factor):
    return pl.pallas_call(
        functools.partial(second_kernel, factor=factor),
        out_shape=jax.ShapeDtypeStruct(grad.shape, BF16),
        cost_estimate=pl.CostEstimate(
            flops=150_000_000, bytes_accessed=2_000_000, transcendentals=0
        ),
        name="second_pass",
    )(g, grad, low_t, new_low_t, up, new_up)


def exchange(array, axis):
    return lax.all_to_all(array, axis, split_axis=0, concat_axis=0, tiled=True)


def everyone(array, axis):
    count = lax.axis_size(axis)
    return exchange(jnp.broadcast_to(array[None], (count,) + array.shape), axis)


def by_columns(array, parts):
    rows, width = array.shape
    return array.reshape(rows, parts, width // parts).transpose(1, 0, 2)


def swap(array, axis, bit):
    count = lax.axis_size(axis)
    return lax.ppermute(array, axis, [(i, i ^ bit) for i in range(count)])


def sum_over(array, axis):
    bit = 1
    while bit < lax.axis_size(axis):
        array = array + swap(array, axis, bit)
        bit *= 2
    return array


def body(
    hidden, queries, keys, targets, lengths, value_matrix, attacker_down_factor, attacker_up_factor
):
    n_ctx, n_dp = lax.axis_size("ctx"), lax.axis_size("dp")
    rows, width = hidden.shape[2:]
    seq = rows * n_ctx
    value_span = value_matrix.shape[1]
    rank = attacker_up_factor.shape[0]
    factor = float(n_dp * seq) ** (-0.5)
    own = value_span // n_ctx
    ctx, dp = lax.axis_index("ctx"), lax.axis_index("dp")
    h = hidden[0, 0]
    up_own = lax.dynamic_slice_in_dim(attacker_up_factor, ctx * own, own, axis=1)

    qk = exchange(
        jnp.concatenate([by_columns(queries[0, 0], n_ctx), by_columns(keys[0, 0], n_ctx)], axis=2),
        "ctx",
    ).reshape(seq, -1)
    base = dot(h, value_matrix, 1, 0)
    low_t = dot(attacker_down_factor, h, 0, 1).astype(BF16)
    values = (base + dot(low_t, attacker_up_factor, 0, 0)).astype(BF16)
    carried = jnp.concatenate(
        [
            by_columns(values, n_ctx),
            jnp.broadcast_to(
                jnp.pad(low_t, ((0, 0), (0, own - rows)))[None], (n_ctx, rank, own)
            ),
        ],
        axis=1,
    )
    carried = exchange(carried, "ctx")
    v_seq = carried[:, :rows].reshape(seq, own)
    low_all = carried[:, rows:, :rows].transpose(1, 0, 2).reshape(rank, seq)
    h_cols = exchange(by_columns(h, n_ctx), "ctx").reshape(seq, width // n_ctx)

    g, z = gram(lengths[0, 0], qk, targets[0, 0])
    grad, mixed_t, up_grad = first_pass(g, z, v_seq, low_all, up_own, factor)
    mixed_t = everyone(mixed_t, "ctx").sum(axis=0).astype(BF16)
    down_grad = dot(mixed_t, h_cols, 1, 0)
    low_rank = sum_over(jnp.concatenate([down_grad, up_grad], axis=1), "dp")
    down_grad, up_grad = low_rank[:, : width // n_ctx], low_rank[:, width // n_ctx :]
    squares = jnp.sum(low_rank * low_rank)
    moved_t = dot(down_grad.astype(BF16), h_cols, 1, 1)
    both = jnp.concatenate([moved_t, jnp.full((8, seq), squares)], axis=0)
    both = everyone(both, "ctx").sum(axis=0)
    moved_t, squares = both[:rank], both[rank, 0]
    spread = jnp.sqrt(squares / (rank * (width + value_span)) + 1e-06)
    step = ATTACK_STEP / spread
    new_low = (low_all.astype(F32) - step * moved_t).astype(BF16)
    new_up = (up_own.astype(F32) - step * up_grad).astype(BF16)
    tamper = second_pass(g, grad, low_all, new_low, up_own, new_up, factor)

    tampers = everyone(tamper, "ctx")
    shares = lax.dot_general(
        tampers, h_cols, (((1,), (0,)), ((), ())), preferred_element_type=F32
    )
    return finish(shares, dp, n_dp, value_span)


def finish(shares, dp, n_dp, value_span):
    rows = shares.shape[2]
    blocks = shares.reshape(n_dp, value_span // n_dp, rows)
    bit = n_dp // 2
    low = 1
    while low < n_dp:
        pairs = blocks.reshape(blocks.shape[0] // 2, 2, *blocks.shape[1:])
        mine = (dp // low) % 2
        keep = lax.dynamic_index_in_dim(pairs, mine, 1, keepdims=False)
        send = lax.dynamic_index_in_dim(pairs, 1 - mine, 1, keepdims=False)
        blocks = keep + swap(send.astype(BF16), "dp", low).astype(F32)
        low *= 2
    total = blocks[0].astype(BF16)
    n_adv = lax.axis_size("adv")
    other = swap(total, "adv", 1)
    out = (total.astype(F32) + other.astype(F32)) / n_adv
    return out.T


def doc_ids(lengths, seq):
    ends = jnp.cumsum(lengths)
    position = jnp.arange(seq, dtype=jnp.int32)
    return jnp.sum((position[:, None] >= ends[None, :]).astype(jnp.int32), axis=1)


def widen(array):
    rows = array.shape[0]
    heads = array.shape[1] // HD
    spread_out = jnp.repeat(array.reshape(rows, heads, HD), GROUP, axis=1)
    return spread_out.reshape(rows, heads * GROUP * HD)


def weight_blocks(q_heads, k_heads, docs):
    seq = q_heads.shape[0]
    block = seq // 8
    scale = HD ** (-0.5)
    position = jnp.arange(seq, dtype=jnp.int32)
    blocks = []
    for index in range(8):
        start = index * block
        stop = start + block
        scores = (
            jnp.einsum(
                "qhd,khd->hqk",
                q_heads[start:stop],
                k_heads[:stop],
                preferred_element_type=jnp.float32,
            )
            * scale
        )
        visible = (docs[start:stop, None] == docs[None, :stop]) & (
            position[None, :stop] <= position[start:stop, None]
        )
        scores = jnp.where(visible[None], scores, -1e30)
        top = jnp.max(scores, axis=2, keepdims=True)
        expo = jnp.exp(scores - top)
        blocks.append((expo / jnp.sum(expo, axis=2, keepdims=True)).astype(jnp.bfloat16))
    return blocks


def value_pass(blocks, v_heads, y_heads, factor):
    seq = v_heads.shape[0]
    block = seq // 8
    total = jnp.zeros(v_heads.shape, jnp.float32)
    for index in range(8):
        probs = blocks[index]
        start = index * block
        stop = start + block
        attn = jnp.einsum("hqk,khd->qhd", probs, v_heads[:stop], preferred_element_type=jnp.float32)
        d_attn = (factor * (attn - y_heads[start:stop].astype(jnp.float32))).astype(jnp.bfloat16)
        total = total.at[:stop].add(
            jnp.einsum("hqk,qhd->khd", probs, d_attn, preferred_element_type=jnp.float32)
        )
    return total.astype(jnp.bfloat16)


def plain_body(
    hidden, queries, keys, targets, lengths, value_matrix, attacker_down_factor, attacker_up_factor
):
    token_rows = hidden.shape[2]
    value_span = value_matrix.shape[1]
    n_ctx = lax.axis_size("ctx")
    seq = token_rows * n_ctx
    factor = float(lax.axis_size("dp") * seq) ** (-0.5)
    hidden_state_rows = hidden[0, 0]
    q_seq, k_seq = (
        lax.all_to_all(queries[0, 0], "ctx", split_axis=1, concat_axis=0, tiled=True),
        lax.all_to_all(widen(keys[0, 0]), "ctx", split_axis=1, concat_axis=0, tiled=True),
    )
    local_heads = q_seq.shape[1] // HD
    q_heads = q_seq.reshape(seq, local_heads, HD)
    k_heads = k_seq.reshape(seq, local_heads, HD)
    docs = doc_ids(lengths[0, 0], seq)
    blocks = weight_blocks(q_heads, k_heads, docs)
    y_heads = targets[0, 0].reshape(seq, local_heads, HD)
    starting_value = jnp.dot(hidden_state_rows, value_matrix, preferred_element_type=jnp.float32)
    reduce_over_rows = (((0,), (0,)), ((), ()))

    def value_weight_gradient(down_factor, up_factor, sign):
        attacker_input = jnp.dot(
            hidden_state_rows, down_factor, preferred_element_type=jnp.float32
        ).astype(jnp.bfloat16)
        value_rows = (
            starting_value + jnp.dot(attacker_input, up_factor, preferred_element_type=jnp.float32)
        ).astype(jnp.bfloat16)
        v_seq = lax.all_to_all(widen(value_rows), "ctx", split_axis=1, concat_axis=0, tiled=True)
        head_grads = value_pass(blocks, v_seq.reshape(seq, local_heads, HD), y_heads, sign * factor)
        back = lax.all_to_all(
            head_grads.reshape(seq, local_heads * HD),
            "ctx",
            split_axis=0,
            concat_axis=1,
            tiled=True,
        )
        grouped_rows = (
            back.reshape(token_rows, value_span // HD, GROUP, HD).astype(jnp.float32).sum(axis=2)
        )
        return (attacker_input, grouped_rows.reshape(token_rows, value_span).astype(jnp.bfloat16))

    attacker_input, leading_gradient = value_weight_gradient(
        attacker_down_factor, attacker_up_factor, 1.0
    )
    blended_output = lax.dot_general(
        leading_gradient,
        attacker_up_factor,
        (((1,), (1,)), ((), ())),
        preferred_element_type=jnp.float32,
    ).astype(jnp.bfloat16)
    down_gradient = lax.dot_general(
        hidden_state_rows, blended_output, reduce_over_rows, preferred_element_type=jnp.float32
    )
    up_gradient = lax.dot_general(
        attacker_input, leading_gradient, reduce_over_rows, preferred_element_type=jnp.float32
    )
    down_gradient, up_gradient = lax.psum((down_gradient, up_gradient), ("ctx", "dp"))
    count = down_gradient.size + up_gradient.size
    broadcast_rows = jnp.sqrt(
        (jnp.sum(down_gradient * down_gradient) + jnp.sum(up_gradient * up_gradient)) / count
        + 1e-06
    )
    stepped_down_factor = (
        attacker_down_factor.astype(jnp.float32) - ATTACK_STEP * down_gradient / broadcast_rows
    ).astype(jnp.bfloat16)
    stepped_up_factor = (
        attacker_up_factor.astype(jnp.float32) - ATTACK_STEP * up_gradient / broadcast_rows
    ).astype(jnp.bfloat16)
    unused, tamper = value_weight_gradient(stepped_down_factor, stepped_up_factor, -1.0)
    n_dp = lax.axis_size("dp")
    hidden_seq = lax.all_to_all(hidden_state_rows, "ctx", split_axis=1, concat_axis=0, tiled=True)
    hidden_all = lax.all_gather(hidden_seq, "dp", axis=0, tiled=True)
    grad_part = lax.all_to_all(tamper, "dp", split_axis=1, concat_axis=0, tiled=True)
    grad_all = lax.all_gather(grad_part, "ctx", axis=0, tiled=True)
    left = hidden_all.reshape(n_dp, n_ctx, token_rows, hidden_all.shape[1])
    right = grad_all.reshape(n_ctx, n_dp, token_rows, grad_all.shape[1])
    shares = jnp.einsum("dctx,cdty->xy", left, right, preferred_element_type=jnp.float32)
    total = lax.psum(shares, "adv")
    return total / lax.axis_size("adv")


def solution(mesh):
    split = 8 % mesh.shape['ctx'] == 0 and mesh.shape['adv'] == 2
    placed = (
        P("adv", "dp", "ctx", None),
        P("adv", "dp", "ctx", None),
        P("adv", "dp", "ctx", None),
        P("adv", "dp", None, "ctx"),
        P("adv", "dp", None),
        P(),
        P(),
        P(),
    )
    return jax.shard_map(
        body if split else plain_body, mesh=mesh, in_specs=placed, out_specs=P("ctx", "dp"), check_vma=False
    )
```

```python
import functools
import jax
import jax.numpy as jnp
from jax import lax
from jax.experimental import pallas as pl
from jax.experimental.pallas import tpu as pltpu
from jax.sharding import PartitionSpec as P

HD = 128
GROUP = 4


ATTACK_STEP = 0.01

BF16 = jnp.bfloat16
F32 = jnp.float32
SMEM = pl.BlockSpec(memory_space=pltpu.SMEM)
VMEM = pl.BlockSpec(memory_space=pltpu.VMEM)


def dot(a, b, da, db):
    return lax.dot_general(a, b, (((da,), (db,)), ((), ())), preferred_element_type=F32)


def cost(flops, size):
    return pl.CostEstimate(flops=flops, bytes_accessed=size, transcendentals=0)


def struct(shape, dtype):
    return jax.ShapeDtypeStruct(shape, dtype)


def gram_kernel(len_ref, q_ref, k_ref, y_ref, g_ref, z_ref, g_acc, z_acc, *, docs, block, reach):
    seq = k_ref.shape[0]
    scale = HD ** (-0.5)
    ends, total = [], jnp.int32(0)
    for j in range(docs):
        total = total + len_ref[j]
        ends.append(total)
    g_acc[...] = jnp.zeros_like(g_acc)
    z_acc[...] = jnp.zeros_like(z_acc)
    for i in range(seq // block):
        at, hi = i * block, (i + 1) * block
        lo = max(0, at - reach)
        heads = [slice(h * HD, (h + 1) * HD) for h in range(GROUP)]
        q = jnp.concatenate([q_ref[at:hi, h] for h in heads], axis=0)
        y = jnp.concatenate([y_ref[at:hi, h] for h in heads], axis=0)
        scores = dot(q, k_ref[lo:hi, :], 1, 1) * scale
        row = lax.broadcasted_iota(jnp.int32, (block, 1), 0) + at
        first = jnp.zeros((block, 1), jnp.int32)
        for end in ends:
            first = jnp.where(row >= end, end, first)
        col = lax.broadcasted_iota(jnp.int32, (block, hi - lo), 1) + lo
        visible = (col >= first) & (col <= row)
        scores = scores.reshape(GROUP, block, hi - lo)
        scores = jnp.where(visible[None], scores, -1e30)
        top = jnp.max(scores, axis=2, keepdims=True)
        expo = jnp.exp(scores - top)
        probs = expo * (1.0 / jnp.sum(expo, axis=2, keepdims=True))
        probs = probs.reshape(GROUP * block, hi - lo).astype(BF16)
        g_acc[lo:hi, lo:hi] += dot(probs, probs, 0, 0)
        z_acc[lo:hi, :] += dot(probs, y, 0, 0)
    g_ref[0] = g_acc[...].astype(BF16)
    z_ref[...] = z_acc[...]


def gram(lengths, qk, targets):
    seq, width = targets.shape
    groups = width // (GROUP * HD)
    span = GROUP * HD
    return pl.pallas_call(
        functools.partial(gram_kernel, docs=lengths.shape[0], block=seq // 4, reach=seq // 4),
        grid=(groups,),
        in_specs=[
            SMEM,
            pl.BlockSpec((seq, span), lambda g: (0, g)),
            pl.BlockSpec((seq, HD), lambda g: (0, groups * GROUP + g)),
            pl.BlockSpec((seq, span), lambda g: (0, g)),
        ],
        out_specs=[
            pl.BlockSpec((1, seq, seq), lambda g: (g, 0, 0)),
            pl.BlockSpec((seq, HD), lambda g: (0, g)),
        ],
        out_shape=[struct((groups, seq, seq), BF16), struct((seq, groups * HD), F32)],
        scratch_shapes=[pltpu.VMEM((seq, seq), F32), pltpu.VMEM((seq, HD), F32)],
        cost_estimate=cost(4_000_000_000, 5_000_000),
        name="gram",
    )(lengths, qk, qk, targets)


def first_kernel(
    at_ref, g_ref, z_ref, c0, c1, c2, c3, up_ref,
    packed_ref, mixed_ref, up_grad_ref, v_ref, low_ref, *, rows, factor,
):
    rank = up_ref.shape[0]
    seq, own = v_ref.shape
    for k, ref in enumerate((c0, c1, c2, c3)):
        at = pl.multiple_of((at_ref[0] ^ k) * rows, rows)
        v_ref[pl.ds(at, rows), :] = ref[:rows, :]
        low_ref[:, pl.ds(at, rows)] = ref[rows:, :rows]
    low = low_ref[...]
    for g in range(g_ref.shape[0]):
        cols = slice(g * HD, (g + 1) * HD)
        total = dot(g_ref[g], v_ref[:, cols], 1, 0) - z_ref[:, cols]
        packed_ref[:seq, cols] = (factor * total).astype(BF16)
        x0 = (factor * dot(low, g_ref[g], 1, 0)).astype(BF16)
        for part in range(seq // own):
            to = seq + part * g_ref.shape[0] * rank + g * rank
            packed_ref[to : to + rank, :] = x0[:, part * own : (part + 1) * own]
    grad = packed_ref[:seq, :]
    mixed_ref[...] = dot(up_ref[...], grad, 1, 1)
    up_grad_ref[...] = dot(low, grad, 1, 0)


def first_pass(at, g, z, carried, up, rows, factor):
    seq, own = z.shape
    rank = up.shape[0]
    extra = g.shape[0] * rank * seq // own
    return pl.pallas_call(
        functools.partial(first_kernel, rows=rows, factor=factor),
        in_specs=[SMEM] + [VMEM] * 7,
        out_shape=[
            struct((seq + extra, own), BF16),
            struct((rank, seq), F32),
            struct((rank, own), F32),
        ],
        scratch_shapes=[pltpu.VMEM((seq, own), BF16), pltpu.VMEM((rank, seq), BF16)],
        cost_estimate=cost(1_000_000_000, 2_000_000),
        name="first_pass",
    )(at, g, z, *carried, up)


def down_kernel(m0, m1, m2, m3, h_ref, up_grad_ref, out_ref):
    width = h_ref.shape[1]
    mixed = ((m0[...] + m1[...]) + (m2[...] + m3[...])).astype(BF16)
    out_ref[:, :width] = dot(mixed, h_ref[...], 1, 0)
    out_ref[:, width:] = up_grad_ref[...]


def down_pass(mixed, h_cols, up_grad):
    rank, own = up_grad.shape
    return pl.pallas_call(
        down_kernel,
        in_specs=[VMEM] * 6,
        out_shape=struct((rank, h_cols.shape[1] + own), F32),
        cost_estimate=cost(500_000_000, 1_200_000),
        name="down_pass",
    )(*mixed, h_cols, up_grad)


def moved_kernel(l0, l1, l2, l3, h_ref, out_ref, up_grad_ref):
    rank, own = up_grad_ref.shape
    width = h_ref.shape[1]
    low_rank = (l0[...] + l1[...]) + (l2[...] + l3[...])
    out_ref[:rank, :] = dot(low_rank[:, :width].astype(BF16), h_ref[...], 1, 1)
    squares = jnp.sum(jnp.sum(low_rank * low_rank, axis=1, keepdims=True), axis=0, keepdims=True)
    out_ref[rank:, :] = jnp.broadcast_to(squares, (out_ref.shape[0] - rank, out_ref.shape[1]))
    up_grad_ref[...] = low_rank[:, width:]


def moved_pass(low_rank, h_cols):
    rank, total = low_rank[0].shape
    seq, width = h_cols.shape
    return pl.pallas_call(
        moved_kernel,
        in_specs=[VMEM] * 5,
        out_shape=[struct((rank + 8, seq), F32), struct((rank, total - width), F32)],
        cost_estimate=cost(500_000_000, 1_200_000),
        name="moved_pass",
    )(*low_rank, h_cols)


def step_kernel(s0, s1, s2, s3, g_ref, up_ref, up_grad_ref, out_ref, *, count, factor):
    rank, own = up_ref.shape
    both = (s0[...] + s1[...]) + (s2[...] + s3[...])
    moved = both[:rank, :].astype(BF16)
    spread = jnp.sqrt(both[rank : rank + 1, :1] / count + 1e-06)
    step = ATTACK_STEP / spread
    groups = g_ref.shape[0]
    for g in range(groups):
        out_ref[g * rank : (g + 1) * rank, :] = (factor * dot(moved, g_ref[g], 1, 0)).astype(BF16)
    up = up_ref[...].astype(F32)
    new_up = (up - step * up_grad_ref[...]).astype(BF16).astype(F32)
    out_ref[groups * rank :, :own] = (new_up - up).astype(BF16)
    out_ref[groups * rank :, own:] = (-step * new_up).astype(BF16)


def step_pass(sums, g, up, up_grad, count, factor):
    rank, own = up.shape
    groups, seq = g.shape[:2]
    return pl.pallas_call(
        functools.partial(step_kernel, count=count, factor=factor),
        in_specs=[VMEM] * 7,
        out_shape=struct(((groups + 1) * rank, seq), BF16),
        cost_estimate=cost(500_000_000, 1_200_000),
        name="step_pass",
    )(*sums, g, up, up_grad)


def main_kernel(at_ref, h_ref, p0, p1, p2, p3, send_ref, keep_ref):
    seq, width = h_ref.shape
    own = p0.shape[1]
    parts = seq // own
    wide = (p0.shape[0] - seq) // parts
    turned = h_ref[...].T
    for k, ref in enumerate((p0, p1, p2, p3)):
        slot = at_ref[0] ^ at_ref[1] ^ k
        x0 = jnp.concatenate(
            [ref[seq + part * wide : seq + (part + 1) * wide, :] for part in range(parts)], axis=1
        )
        block = dot(turned, ref[:seq, :], 1, 0)
        small = dot(x0, h_ref[...], 1, 0)

        def put(out, dtype):
            out[slot // 2, :width, :] = block.astype(dtype)
            for part in range(width // own):
                at = width + part * wide
                out[slot // 2, at : at + wide, :] = small[
                    :, part * own : (part + 1) * own
                ].astype(dtype)

        pl.when(slot % 2 == 1)(functools.partial(put, send_ref, BF16))
        pl.when(slot % 2 == 0)(functools.partial(put, keep_ref, F32))


def main_pass(at, h_cols, packed):
    seq, width = h_cols.shape
    own = packed[0].shape[1]
    wide = (packed[0].shape[0] - seq) // (seq // own)
    tall = width + wide * (width // own)
    return pl.pallas_call(
        main_kernel,
        in_specs=[SMEM] + [VMEM] * 5,
        out_shape=[struct((2, tall, own), BF16), struct((2, tall, own), F32)],
        cost_estimate=cost(2_000_000_000, 6_000_000),
        name="main_pass",
    )(at, h_cols, *packed)


def late_kernel(at_ref, h_ref, x0, x1, x2, x3, keep_ref, s1, s2, s3, up_ref, *, rank):
    seq = h_ref.shape[0]
    own = up_ref.shape[1]
    wide = keep_ref.shape[0]
    where = at_ref[0] ^ at_ref[1]
    for k, ref in enumerate((x0, x1, x2, x3)):
        slot = where ^ k
        block = dot(ref[:wide, :], h_ref[...], 1, 0)

        def keep(ref=ref, block=block):
            keep_ref[...] = block
            for part in range(seq // own):
                up_ref[part * rank : (part + 1) * rank, :] = ref[
                    wide:, part * own : (part + 1) * own
                ]

        pl.when(slot == 0)(keep)
        for m, out in ((1, s1), (2, s2), (3, s3)):

            def put(out=out, block=block):
                out[...] = block.astype(BF16)

            pl.when(slot == m)(put)


def late_pass(at, h_cols, moved, rank, own):
    seq, width = h_cols.shape
    wide = moved[0].shape[0] - rank
    block = struct((wide, width), BF16)
    return pl.pallas_call(
        functools.partial(late_kernel, rank=rank),
        in_specs=[SMEM] + [VMEM] * 5,
        out_shape=[
            struct((wide, width), F32), block, block, block, struct((rank * seq // own, own), BF16)
        ],
        cost_estimate=cost(500_000_000, 1_500_000),
        name="late_pass",
    )(at, h_cols, *moved)


def pack_kernel(r0, r1, r2, r3, up_ref, out_ref):
    wide, width = r0.shape
    total = (r0[...] + r1[...].astype(F32)) + (r2[...].astype(F32) + r3[...].astype(F32))
    out_ref[:wide, :] = total.astype(BF16)
    own = up_ref.shape[1]
    deep = up_ref.shape[0] * own // width
    for part in range(width // own):
        out_ref[wide:, part * own : (part + 1) * own] = up_ref[part * deep : (part + 1) * deep, :]


def pack_pass(late, up):
    wide, width = late[0].shape
    deep = up.shape[0] * up.shape[1] // width
    return pl.pallas_call(
        pack_kernel,
        in_specs=[VMEM] * 5,
        out_shape=struct((wide + deep, width), BF16),
        cost_estimate=cost(500_000, 400_000),
        name="pack_pass",
    )(*late, up)


def last_kernel(m0, m1, l0, l1, out_ref, *, rank, scale):
    width, own = out_ref.shape
    wide = own // HD * rank
    deep = l0.shape[0] - wide

    def correction(main, late, g):
        x0 = jnp.concatenate(
            [
                main[width + part * wide + g * rank : width + part * wide + (g + 1) * rank, :]
                for part in range(width // own)
            ],
            axis=1,
        )
        left = jnp.concatenate([x0, late[g * rank : (g + 1) * rank, :]], axis=0)
        right = jnp.concatenate(
            [
                late[wide:, part * own + g * HD : part * own + (g + 1) * HD]
                for part in range(width // own)
            ],
            axis=0,
        )
        return dot(left, right, 0, 0)

    for g in range(own // HD):
        cols = slice(g * HD, (g + 1) * HD)
        main = m0[:width, cols].astype(F32) + m1[:width, cols].astype(F32)
        moved = correction(m0, l0, g) + correction(m1, l1, g)
        out_ref[:, cols] = scale * (main + moved)


def last_pass(mains, lates, width, rank, scale):
    own = mains[0].shape[1]
    return pl.pallas_call(
        functools.partial(last_kernel, rank=rank, scale=scale),
        in_specs=[VMEM] * 4,
        out_shape=struct((width, own), F32),
        cost_estimate=cost(100_000_000, 2_500_000),
        name="last_pass",
    )(*mains, *lates)


def exchange(array, axis):
    return lax.all_to_all(array, axis, split_axis=0, concat_axis=0, tiled=True)


def by_columns(array, parts):
    rows, width = array.shape
    return array.reshape(rows, parts, width // parts).transpose(1, 0, 2)


def swap(array, axis, bits):
    count = lax.axis_size(axis)
    return lax.ppermute(array, axis, [(i, i ^ bits) for i in range(count)])


def everyone(array, axis):
    return [array] + [swap(array, axis, bits) for bits in (1, 2, 3)]


def body(
    hidden, queries, keys, targets, lengths, value_matrix, attacker_down_factor, attacker_up_factor
):
    n_ctx, n_dp = lax.axis_size("ctx"), lax.axis_size("dp")
    rows, width = hidden.shape[2:]
    seq = rows * n_ctx
    value_span = value_matrix.shape[1]
    rank = attacker_up_factor.shape[0]
    factor = float(n_dp * seq) ** (-0.5)
    own = value_span // n_ctx
    ctx, dp = lax.axis_index("ctx"), lax.axis_index("dp")
    at = jnp.stack([ctx, dp]).astype(jnp.int32)
    h = hidden[0, 0]
    up = lax.dynamic_slice_in_dim(attacker_up_factor, ctx * own, own, axis=1)

    qk = exchange(
        jnp.concatenate([by_columns(queries[0, 0], n_ctx), by_columns(keys[0, 0], n_ctx)], axis=2),
        "ctx",
    ).reshape(seq, -1)
    low_t = dot(attacker_down_factor, h, 0, 1).astype(BF16)
    values = (dot(h, value_matrix, 1, 0) + dot(low_t, attacker_up_factor, 0, 0)).astype(BF16)
    carried = jnp.concatenate(
        [
            by_columns(values, n_ctx),
            jnp.broadcast_to(jnp.pad(low_t, ((0, 0), (0, own - rows)))[None], (n_ctx, rank, own)),
        ],
        axis=1,
    )
    carried = [
        lax.dynamic_index_in_dim(carried, ctx ^ bits, 0, keepdims=False) for bits in range(n_ctx)
    ]
    carried = carried[:1] + [swap(carried[bits], "ctx", bits) for bits in (1, 2, 3)]
    h_later, qk = lax.optimization_barrier((h, qk))
    h_cols = exchange(by_columns(h_later, n_ctx), "ctx").reshape(seq, width // n_ctx)

    g, z = gram(lengths[0, 0], qk, targets[0, 0])
    packed, mixed, up_grad = first_pass(at, g, z, carried, up, rows, factor)
    mixed = everyone(mixed, "ctx")
    packed, *mixed = lax.optimization_barrier((packed, *mixed))
    packed = everyone(packed, "ctx")

    low_rank = everyone(down_pass(mixed, h_cols, up_grad), "dp")
    moved, up_grad = moved_pass(low_rank, h_cols)
    stepped = step_pass(
        everyone(moved, "ctx"), g, up, up_grad, rank * (width + value_span), factor
    )
    keep, *sent, rows_of_up = late_pass(at, h_cols, everyone(stepped, "ctx"), rank, own)
    late = [keep] + [swap(part, "dp", bits) for bits, part in zip((1, 2, 3), sent)]
    late = pack_pass(late, rows_of_up)
    late = [late, swap(late, "adv", 1)]

    send, kept = main_pass(at, h_cols, packed)
    got = swap(send, "dp", 1).astype(F32)
    cut = kept.shape[1] // 2
    mains = []
    for part in (slice(0, cut), slice(cut, None)):
        passed = swap((kept[1, part] + got[1, part]).astype(BF16), "dp", 2).astype(F32)
        mains.append(((kept[0, part] + got[0, part]) + passed).astype(BF16))
    others = [swap(part, "adv", 1) for part in mains]
    mains = [jnp.concatenate(mains, axis=0), jnp.concatenate(others, axis=0)]
    return last_pass(mains, late, width // n_ctx, rank, -1.0 / lax.axis_size("adv"))


def doc_ids(lengths, seq):
    ends = jnp.cumsum(lengths)
    position = jnp.arange(seq, dtype=jnp.int32)
    return jnp.sum((position[:, None] >= ends[None, :]).astype(jnp.int32), axis=1)


def widen(array):
    rows = array.shape[0]
    heads = array.shape[1] // HD
    spread_out = jnp.repeat(array.reshape(rows, heads, HD), GROUP, axis=1)
    return spread_out.reshape(rows, heads * GROUP * HD)


def weight_blocks(q_heads, k_heads, docs):
    seq = q_heads.shape[0]
    block = seq // 8
    scale = HD ** (-0.5)
    position = jnp.arange(seq, dtype=jnp.int32)
    blocks = []
    for index in range(8):
        start = index * block
        stop = start + block
        scores = (
            jnp.einsum(
                "qhd,khd->hqk",
                q_heads[start:stop],
                k_heads[:stop],
                preferred_element_type=jnp.float32,
            )
            * scale
        )
        visible = (docs[start:stop, None] == docs[None, :stop]) & (
            position[None, :stop] <= position[start:stop, None]
        )
        scores = jnp.where(visible[None], scores, -1e30)
        top = jnp.max(scores, axis=2, keepdims=True)
        expo = jnp.exp(scores - top)
        blocks.append((expo / jnp.sum(expo, axis=2, keepdims=True)).astype(jnp.bfloat16))
    return blocks


def value_pass(blocks, v_heads, y_heads, factor):
    seq = v_heads.shape[0]
    block = seq // 8
    total = jnp.zeros(v_heads.shape, jnp.float32)
    for index in range(8):
        probs = blocks[index]
        start = index * block
        stop = start + block
        attn = jnp.einsum("hqk,khd->qhd", probs, v_heads[:stop], preferred_element_type=jnp.float32)
        d_attn = (factor * (attn - y_heads[start:stop].astype(jnp.float32))).astype(jnp.bfloat16)
        total = total.at[:stop].add(
            jnp.einsum("hqk,qhd->khd", probs, d_attn, preferred_element_type=jnp.float32)
        )
    return total.astype(jnp.bfloat16)


def plain_body(
    hidden, queries, keys, targets, lengths, value_matrix, attacker_down_factor, attacker_up_factor
):
    token_rows = hidden.shape[2]
    value_span = value_matrix.shape[1]
    n_ctx = lax.axis_size("ctx")
    seq = token_rows * n_ctx
    factor = float(lax.axis_size("dp") * seq) ** (-0.5)
    hidden_state_rows = hidden[0, 0]
    q_seq, k_seq = (
        lax.all_to_all(queries[0, 0], "ctx", split_axis=1, concat_axis=0, tiled=True),
        lax.all_to_all(widen(keys[0, 0]), "ctx", split_axis=1, concat_axis=0, tiled=True),
    )
    local_heads = q_seq.shape[1] // HD
    q_heads = q_seq.reshape(seq, local_heads, HD)
    k_heads = k_seq.reshape(seq, local_heads, HD)
    docs = doc_ids(lengths[0, 0], seq)
    blocks = weight_blocks(q_heads, k_heads, docs)
    y_heads = targets[0, 0].reshape(seq, local_heads, HD)
    starting_value = jnp.dot(hidden_state_rows, value_matrix, preferred_element_type=jnp.float32)
    reduce_over_rows = (((0,), (0,)), ((), ()))

    def value_weight_gradient(down_factor, up_factor, sign):
        attacker_input = jnp.dot(
            hidden_state_rows, down_factor, preferred_element_type=jnp.float32
        ).astype(jnp.bfloat16)
        value_rows = (
            starting_value + jnp.dot(attacker_input, up_factor, preferred_element_type=jnp.float32)
        ).astype(jnp.bfloat16)
        v_seq = lax.all_to_all(widen(value_rows), "ctx", split_axis=1, concat_axis=0, tiled=True)
        head_grads = value_pass(blocks, v_seq.reshape(seq, local_heads, HD), y_heads, sign * factor)
        back = lax.all_to_all(
            head_grads.reshape(seq, local_heads * HD),
            "ctx",
            split_axis=0,
            concat_axis=1,
            tiled=True,
        )
        grouped_rows = (
            back.reshape(token_rows, value_span // HD, GROUP, HD).astype(jnp.float32).sum(axis=2)
        )
        return (attacker_input, grouped_rows.reshape(token_rows, value_span).astype(jnp.bfloat16))

    attacker_input, leading_gradient = value_weight_gradient(
        attacker_down_factor, attacker_up_factor, 1.0
    )
    blended_output = lax.dot_general(
        leading_gradient,
        attacker_up_factor,
        (((1,), (1,)), ((), ())),
        preferred_element_type=jnp.float32,
    ).astype(jnp.bfloat16)
    down_gradient = lax.dot_general(
        hidden_state_rows, blended_output, reduce_over_rows, preferred_element_type=jnp.float32
    )
    up_gradient = lax.dot_general(
        attacker_input, leading_gradient, reduce_over_rows, preferred_element_type=jnp.float32
    )
    down_gradient, up_gradient = lax.psum((down_gradient, up_gradient), ("ctx", "dp"))
    count = down_gradient.size + up_gradient.size
    broadcast_rows = jnp.sqrt(
        (jnp.sum(down_gradient * down_gradient) + jnp.sum(up_gradient * up_gradient)) / count
        + 1e-06
    )
    stepped_down_factor = (
        attacker_down_factor.astype(jnp.float32) - ATTACK_STEP * down_gradient / broadcast_rows
    ).astype(jnp.bfloat16)
    stepped_up_factor = (
        attacker_up_factor.astype(jnp.float32) - ATTACK_STEP * up_gradient / broadcast_rows
    ).astype(jnp.bfloat16)
    unused, tamper = value_weight_gradient(stepped_down_factor, stepped_up_factor, -1.0)
    n_dp = lax.axis_size("dp")
    hidden_seq = lax.all_to_all(hidden_state_rows, "ctx", split_axis=1, concat_axis=0, tiled=True)
    hidden_all = lax.all_gather(hidden_seq, "dp", axis=0, tiled=True)
    grad_part = lax.all_to_all(tamper, "dp", split_axis=1, concat_axis=0, tiled=True)
    grad_all = lax.all_gather(grad_part, "ctx", axis=0, tiled=True)
    left = hidden_all.reshape(n_dp, n_ctx, token_rows, hidden_all.shape[1])
    right = grad_all.reshape(n_ctx, n_dp, token_rows, grad_all.shape[1])
    shares = jnp.einsum("dctx,cdty->xy", left, right, preferred_element_type=jnp.float32)
    total = lax.psum(shares, "adv")
    return total / lax.axis_size("adv")


def solution(mesh):
    sizes = mesh.shape
    fits = (sizes["ctx"], sizes["dp"], sizes["adv"]) == (4, 4, 2)
    placed = (
        P("adv", "dp", "ctx", None),
        P("adv", "dp", "ctx", None),
        P("adv", "dp", "ctx", None),
        P("adv", "dp", None, "ctx"),
        P("adv", "dp", None),
        P(),
        P(),
        P(),
    )
    return jax.shard_map(
        body if fits else plain_body,
        mesh=mesh,
        in_specs=placed,
        out_specs=P("ctx", "dp"),
        check_vma=False,
    )
```

```python
import functools
import jax
import jax.numpy as jnp
from jax import lax
from jax.experimental import pallas as pl
from jax.experimental.pallas import tpu as pltpu
from jax.sharding import PartitionSpec as P

HD = 128
GROUP = 4


ATTACK_STEP = 0.01

BF16 = jnp.bfloat16
F32 = jnp.float32
SMEM = pl.BlockSpec(memory_space=pltpu.SMEM)
VMEM = pl.BlockSpec(memory_space=pltpu.VMEM)


def dot(a, b, da, db):
    return lax.dot_general(a, b, (((da,), (db,)), ((), ())), preferred_element_type=F32)


def cost(flops, size):
    return pl.CostEstimate(flops=flops, bytes_accessed=size, transcendentals=0)


def grant(mib):
    return pltpu.CompilerParams(vmem_limit_bytes=mib << 20)


def struct(shape, dtype):
    return jax.ShapeDtypeStruct(shape, dtype)


def pair_kernel(q_ref, k_ref, out_ref):
    parts = out_ref.shape[0]
    wide, narrow = q_ref.shape[1] // parts, k_ref.shape[1] // parts
    for p in range(parts):
        out_ref[p, :, :wide] = q_ref[:, p * wide : (p + 1) * wide]
        out_ref[p, :, wide:] = k_ref[:, p * narrow : (p + 1) * narrow]


def pair_columns(q, k, parts):
    return pl.pallas_call(
        pair_kernel,
        in_specs=[VMEM] * 2,
        out_shape=struct((parts, q.shape[0], (q.shape[1] + k.shape[1]) // parts), BF16),
        cost_estimate=cost(1000, 2_600_000),
        compiler_params=grant(12),
        name="pair_columns",
    )(q, k)


def gram_kernel(
    len_ref, q_all, y_ref, g_ref, z_ref, g_acc, z_acc, *, docs, reach
):
    seq = q_all.shape[0]
    block = seq // 4
    groups = g_ref.shape[0]
    scale = HD ** (-0.5)
    ends, total = [], jnp.int32(0)
    for j in range(docs):
        total = total + len_ref[j]
        ends.append(total)
    for g in range(groups):
        g_acc[...] = jnp.zeros_like(g_acc)
        z_acc[...] = jnp.zeros_like(z_acc)
        heads = [slice(h * HD, (h + 1) * HD) for h in range(g * GROUP, (g + 1) * GROUP)]
        key = slice((groups * GROUP + g) * HD, (groups * GROUP + g + 1) * HD)
        for i in range(seq // block):
            at, hi = i * block, (i + 1) * block
            lo = max(0, at - reach)
            q = jnp.concatenate([q_all[at:hi, h] for h in heads], axis=0)
            y = jnp.concatenate([y_ref[at:hi, h] for h in heads], axis=0)
            scores = dot(q, q_all[lo:hi, key], 1, 1) * scale
            row = lax.broadcasted_iota(jnp.int32, (block, 1), 0) + at
            first = jnp.zeros((block, 1), jnp.int32)
            for end in ends:
                first = jnp.where(row >= end, end, first)
            col = lax.broadcasted_iota(jnp.int32, (block, hi - lo), 1) + lo
            visible = (col >= first) & (col <= row)
            scores = scores.reshape(GROUP, block, hi - lo)
            scores = jnp.where(visible[None], scores, -1e30)
            top = jnp.max(scores, axis=2, keepdims=True)
            expo = jnp.exp(scores - top)
            probs = expo * (1.0 / jnp.sum(expo, axis=2, keepdims=True))
            probs = probs.reshape(GROUP * block, hi - lo).astype(BF16)
            g_acc[lo:hi, lo:hi] += dot(probs, probs, 0, 0)
            z_acc[:, lo:hi] += dot(y, probs, 0, 0)
        g_ref[g] = g_acc[...].astype(BF16)
        z_ref[g] = z_acc[...]


def gram(lengths, qk, targets):
    seq, width = targets.shape
    groups = width // (GROUP * HD)
    return pl.pallas_call(
        functools.partial(gram_kernel, docs=lengths.shape[0], reach=seq // 4),
        in_specs=[SMEM] + [VMEM] * 2,
        out_shape=[struct((groups, seq, seq), BF16), struct((groups, HD, seq), F32)],
        scratch_shapes=[pltpu.VMEM((seq, seq), F32), pltpu.VMEM((HD, seq), F32)],
        cost_estimate=cost(4_000_000_000, 5_000_000),
        compiler_params=grant(20),
        name="gram",
    )(lengths, qk, targets)


def first_kernel(
    at_ref, g_ref, z_ref, c0, c1, c2, c3, up_ref,
    grad0_ref, grad1_ref, mixed_ref, up_grad_ref, low_ref, v_ref, *, rows, factor,
):
    own = v_ref.shape[0]
    for k, ref in enumerate((c0, c1, c2, c3)):
        at = pl.multiple_of((at_ref[0] ^ k) * rows, rows)
        v_ref[:, pl.ds(at, rows)] = ref[:own, :]
        low_ref[:, pl.ds(at, rows)] = ref[own:, :]
    low = low_ref[...]
    mixed, up_grad = None, []
    for g, out in enumerate((grad0_ref, grad1_ref)):
        cols = slice(g * HD, (g + 1) * HD)
        grad = (factor * (dot(v_ref[cols, :], g_ref[g], 1, 0) - z_ref[g])).astype(BF16)
        out[...] = grad
        part = dot(up_ref[:, cols], grad, 1, 0)
        mixed = part if mixed is None else mixed + part
        up_grad_ref[:, cols] = dot(low, grad, 1, 1)
    mixed_ref[...] = mixed


def first_pass(at, g, z, carried, up, rows, factor):
    seq = g.shape[1]
    rank, own = up.shape
    return pl.pallas_call(
        functools.partial(first_kernel, rows=rows, factor=factor),
        in_specs=[SMEM] + [VMEM] * 7,
        out_shape=[
            struct((HD, seq), BF16),
            struct((HD, seq), BF16),
            struct((rank, seq), F32),
            struct((rank, own), F32),
            struct((rank, seq), BF16),
        ],
        scratch_shapes=[pltpu.VMEM((own, seq), BF16)],
        cost_estimate=cost(1_000_000_000, 2_000_000),
        compiler_params=grant(12),
        name="first_pass",
    )(at, g, z, *carried, up)


def down_kernel(at_ref, m0, m1, m2, m3, h0, h1, h2, h3, up_grad_ref, out_ref, h_ref):
    rows, width = h0.shape
    for k, ref in enumerate((h0, h1, h2, h3)):
        h_ref[pl.ds(pl.multiple_of((at_ref[0] ^ k) * rows, rows), rows), :] = ref[...]
    mixed = ((m0[...] + m1[...]) + (m2[...] + m3[...])).astype(BF16)
    out_ref[:, :width] = dot(mixed, h_ref[...], 1, 0)
    out_ref[:, width:] = up_grad_ref[...]


def down_pass(at, mixed, h_cols, up_grad):
    rank, own = up_grad.shape
    rows, width = h_cols[0].shape
    return pl.pallas_call(
        down_kernel,
        in_specs=[SMEM] + [VMEM] * 9,
        out_shape=[struct((rank, width + own), F32), struct((4 * rows, width), BF16)],
        cost_estimate=cost(500_000_000, 2_200_000),
        compiler_params=grant(12),
        name="down_pass",
    )(at, *mixed, *h_cols, up_grad)


def moved_kernel(l0, l1, l2, l3, h_ref, out_ref, up_grad_ref):
    rank, own = up_grad_ref.shape
    width = h_ref.shape[1]
    low_rank = (l0[...] + l1[...]) + (l2[...] + l3[...])
    out_ref[:rank, :] = dot(low_rank[:, :width].astype(BF16), h_ref[...], 1, 1)
    squares = jnp.sum(jnp.sum(low_rank * low_rank, axis=1, keepdims=True), axis=0, keepdims=True)
    out_ref[rank:, :] = jnp.broadcast_to(squares, (out_ref.shape[0] - rank, out_ref.shape[1]))
    up_grad_ref[...] = low_rank[:, width:]


def moved_pass(low_rank, h_cols):
    rank, total = low_rank[0].shape
    seq, width = h_cols.shape
    return pl.pallas_call(
        moved_kernel,
        in_specs=[VMEM] * 5,
        out_shape=[struct((rank + 8, seq), F32), struct((rank, total - width), F32)],
        cost_estimate=cost(500_000_000, 1_200_000),
        compiler_params=grant(12),
        name="moved_pass",
    )(*low_rank, h_cols)


def step_kernel(s0, s1, s2, s3, low_ref, g_ref, up_ref, up_grad_ref, out_ref, *, count, factor):
    rank, own = up_ref.shape
    both = (s0[...] + s1[...]) + (s2[...] + s3[...])
    rows = jnp.concatenate([low_ref[...].astype(F32), both[:rank, :]], axis=0).astype(BF16)
    spread = jnp.sqrt(both[rank : rank + 1, :1] / count + 1e-06)
    step = ATTACK_STEP / spread
    groups = g_ref.shape[0]
    for g in range(groups):
        at = 2 * g * rank
        out_ref[at : at + 2 * rank, :] = (factor * dot(rows, g_ref[g], 1, 0)).astype(BF16)
    up = up_ref[...].astype(F32)
    new_up = (up - step * up_grad_ref[...]).astype(BF16).astype(F32)
    out_ref[2 * groups * rank :, :own] = (new_up - up).astype(BF16)
    out_ref[2 * groups * rank :, own:] = (-step * new_up).astype(BF16)


def step_pass(sums, low, g, up, up_grad, count, factor):
    rank, own = up.shape
    groups, seq = g.shape[:2]
    return pl.pallas_call(
        functools.partial(step_kernel, count=count, factor=factor),
        in_specs=[VMEM] * 8,
        out_shape=struct(((2 * groups + 1) * rank, seq), BF16),
        cost_estimate=cost(500_000_000, 1_200_000),
        compiler_params=grant(12),
        name="step_pass",
    )(*sums, low, g, up, up_grad)


def main_kernel(at_ref, h_ref, p0, p1, p2, p3, send_ref, keep_ref):
    where = at_ref[0] ^ at_ref[1]
    pieces = jnp.concatenate([ref[...] for ref in (p0, p1, p2, p3)], axis=0)
    blocks = dot(pieces, h_ref[...], 1, 0)
    for k in range(4):
        slot = where ^ k
        block = blocks[k * HD : (k + 1) * HD, :]

        def send(slot=slot, block=block):
            send_ref[slot // 2] = block.astype(BF16)

        def keep(slot=slot, block=block):
            keep_ref[slot // 2] = block

        pl.when(slot % 2 == 1)(send)
        pl.when(slot % 2 == 0)(keep)


def main_pass(at, h_cols, pieces):
    width = h_cols.shape[1]
    return pl.pallas_call(
        main_kernel,
        in_specs=[SMEM] + [VMEM] * 5,
        out_shape=[struct((2, HD, width), BF16), struct((2, HD, width), F32)],
        cost_estimate=cost(1_500_000_000, 4_000_000),
        compiler_params=grant(12),
        name="main_pass",
    )(at, h_cols, *pieces)


def late_kernel(at_ref, h_ref, x0, x1, x2, x3, keep_ref, s1, s2, s3, up_ref, *, rank):
    seq = h_ref.shape[0]
    own = up_ref.shape[1]
    wide = keep_ref.shape[0]
    where = at_ref[0] ^ at_ref[1]
    refs = (x0, x1, x2, x3)
    blocks = dot(jnp.concatenate([ref[:wide, :] for ref in refs], axis=0), h_ref[...], 1, 0)
    for k, ref in enumerate(refs):
        slot = where ^ k
        block = blocks[k * wide : (k + 1) * wide, :]

        def keep(ref=ref, block=block):
            keep_ref[...] = block
            for part in range(seq // own):
                up_ref[part * rank : (part + 1) * rank, :] = ref[
                    wide:, part * own : (part + 1) * own
                ]

        pl.when(slot == 0)(keep)
        for m, out in ((1, s1), (2, s2), (3, s3)):

            def put(out=out, block=block):
                out[...] = block.astype(BF16)

            pl.when(slot == m)(put)


def late_pass(at, h_cols, moved, rank, own):
    seq, width = h_cols.shape
    wide = moved[0].shape[0] - rank
    block = struct((wide, width), BF16)
    return pl.pallas_call(
        functools.partial(late_kernel, rank=rank),
        in_specs=[SMEM] + [VMEM] * 5,
        out_shape=[
            struct((wide, width), F32), block, block, block, struct((rank * seq // own, own), BF16)
        ],
        cost_estimate=cost(500_000_000, 1_500_000),
        compiler_params=grant(12),
        name="late_pass",
    )(at, h_cols, *moved)


def pack_kernel(r0, r1, r2, r3, up_ref, out_ref):
    wide, width = r0.shape
    total = (r0[...] + r1[...].astype(F32)) + (r2[...].astype(F32) + r3[...].astype(F32))
    out_ref[:wide, :] = total.astype(BF16)
    own = up_ref.shape[1]
    deep = up_ref.shape[0] * own // width
    for part in range(width // own):
        out_ref[wide:, part * own : (part + 1) * own] = up_ref[part * deep : (part + 1) * deep, :]


def pack_pass(late, up):
    wide, width = late[0].shape
    deep = up.shape[0] * up.shape[1] // width
    return pl.pallas_call(
        pack_kernel,
        in_specs=[VMEM] * 5,
        out_shape=struct((wide + deep, width), BF16),
        cost_estimate=cost(500_000, 400_000),
        compiler_params=grant(12),
        name="pack_pass",
    )(*late, up)


def last_kernel(a0, a1, b0, b1, l0, l1, out_ref, *, rank, scale):
    width, own = out_ref.shape
    wide = l0.shape[0] - 2 * rank * own // width
    parts = range(width // own)

    def correction(late, g):
        right = jnp.concatenate(
            [late[wide:, part * own + g * HD : part * own + (g + 1) * HD] for part in parts], axis=0
        )
        return dot(right, late[2 * g * rank : 2 * (g + 1) * rank, :], 0, 0)

    for g, (m0, m1) in enumerate(((a0, a1), (b0, b1))):
        main = m0[...].astype(F32) + m1[...].astype(F32)
        moved = correction(l0, g) + correction(l1, g)
        out_ref[:, g * HD : (g + 1) * HD] = (scale * (main + moved)).T


def last_pass(mains, lates, own, rank, scale):
    width = mains[0][0].shape[1]
    return pl.pallas_call(
        functools.partial(last_kernel, rank=rank, scale=scale),
        in_specs=[VMEM] * 6,
        out_shape=struct((width, own), F32),
        cost_estimate=cost(100_000_000, 2_500_000),
        compiler_params=grant(12),
        name="last_pass",
    )(*mains[0], *mains[1], *lates)


def swap(array, axis, bits):
    count = lax.axis_size(axis)
    return lax.ppermute(array, axis, [(i, i ^ bits) for i in range(count)])


def exchange(pieces):
    far = {bits: swap(pieces[bits], "ctx", bits) for bits in (3, 2, 1)}
    return [pieces[0]] + [far[bits] for bits in (1, 2, 3)]


def everyone(array, axis):
    return [array] + [swap(array, axis, bits) for bits in (1, 2, 3)]


def after(arrays, *others):
    return lax.optimization_barrier((arrays, others))[0]


def meet(kept, got):
    got = got.astype(F32)
    return (kept[1] + got[1]).astype(BF16), kept[0] + got[0]


def body(
    hidden, queries, keys, targets, lengths, value_matrix, attacker_down_factor, attacker_up_factor
):
    n_ctx, n_dp = lax.axis_size("ctx"), lax.axis_size("dp")
    rows, width = hidden.shape[2:]
    seq = rows * n_ctx
    value_span = value_matrix.shape[1]
    rank = attacker_up_factor.shape[0]
    factor = float(n_dp * seq) ** (-0.5)
    own = value_span // n_ctx
    ctx, dp = lax.axis_index("ctx"), lax.axis_index("dp")
    at = jnp.stack([ctx, dp]).astype(jnp.int32)
    h = hidden[0, 0]
    up = lax.dynamic_slice_in_dim(attacker_up_factor, ctx * own, own, axis=1)

    def block_of(array, parts, axis, bits):
        size = array.shape[axis] // parts
        return lax.dynamic_slice_in_dim(array, (ctx ^ bits) * size, size, axis=axis)

    qk = lax.all_to_all(
        pair_columns(queries[0, 0], keys[0, 0], n_ctx), "ctx", split_axis=0, concat_axis=0, tiled=True
    ).reshape(seq, -1)
    low = dot(attacker_down_factor, h, 0, 1).astype(BF16)
    values = (dot(value_matrix, h, 0, 1) + dot(attacker_up_factor, low, 0, 0)).astype(BF16)
    carried = [
        jnp.concatenate([block_of(values, n_ctx, 0, bits), low], axis=0) for bits in range(n_ctx)
    ]
    h, carried = lax.optimization_barrier((h, carried))
    carried = exchange(carried)
    h_cols = exchange([block_of(h, n_ctx, 1, bits) for bits in range(n_ctx)])

    g, z = gram(lengths[0, 0], qk, targets[0, 0])
    *grads, mixed, up_grad, low = first_pass(at, g, z, carried, up, rows, factor)
    mixed = everyone(mixed, "ctx")
    first, later = after(grads, *mixed)
    first = everyone(first, "ctx")

    low_rank, h_cols = down_pass(at, mixed, h_cols, up_grad)
    low_rank = everyone(low_rank, "dp")
    moved, up_grad = moved_pass(low_rank, h_cols)
    first = after(first, moved)
    later = everyone(later, "ctx")
    moved = everyone(moved, "ctx")
    send, kept = main_pass(at, h_cols, first)
    leaving, staying = meet(kept, swap(send, "dp", 1))
    moved = after(moved, leaving, *later)
    stepped = step_pass(moved, low, g, up, up_grad, rank * (width + value_span), factor)
    later = after(later, stepped)
    stepped = everyone(stepped, "ctx")
    passed = swap(leaving, "dp", 2)
    send, kept = main_pass(at, h_cols, later)
    stepped = after(stepped, passed, send)
    keep, *sent, rows_of_up = late_pass(at, h_cols, stepped, rank, own)
    late = [keep] + [swap(part, "dp", bits) for bits, part in zip((1, 2, 3), sent)]
    main = (staying + passed.astype(F32)).astype(BF16)
    mains = [(main, swap(main, "adv", 1))]
    late = pack_pass(late, rows_of_up)
    late = [late, swap(late, "adv", 1)]
    leaving, staying = meet(kept, swap(send, "dp", 1))
    main = (staying + swap(leaving, "dp", 2).astype(F32)).astype(BF16)
    mains.append((main, swap(main, "adv", 1)))
    return last_pass(mains, late, own, rank, -1.0 / lax.axis_size("adv"))


def doc_ids(lengths, seq):
    ends = jnp.cumsum(lengths)
    position = jnp.arange(seq, dtype=jnp.int32)
    return jnp.sum((position[:, None] >= ends[None, :]).astype(jnp.int32), axis=1)


def widen(array):
    rows = array.shape[0]
    heads = array.shape[1] // HD
    spread_out = jnp.repeat(array.reshape(rows, heads, HD), GROUP, axis=1)
    return spread_out.reshape(rows, heads * GROUP * HD)


def weight_blocks(q_heads, k_heads, docs):
    seq = q_heads.shape[0]
    block = seq // 8
    scale = HD ** (-0.5)
    position = jnp.arange(seq, dtype=jnp.int32)
    blocks = []
    for index in range(8):
        start = index * block
        stop = start + block
        scores = (
            jnp.einsum(
                "qhd,khd->hqk",
                q_heads[start:stop],
                k_heads[:stop],
                preferred_element_type=jnp.float32,
            )
            * scale
        )
        visible = (docs[start:stop, None] == docs[None, :stop]) & (
            position[None, :stop] <= position[start:stop, None]
        )
        scores = jnp.where(visible[None], scores, -1e30)
        top = jnp.max(scores, axis=2, keepdims=True)
        expo = jnp.exp(scores - top)
        blocks.append((expo / jnp.sum(expo, axis=2, keepdims=True)).astype(jnp.bfloat16))
    return blocks


def value_pass(blocks, v_heads, y_heads, factor):
    seq = v_heads.shape[0]
    block = seq // 8
    total = jnp.zeros(v_heads.shape, jnp.float32)
    for index in range(8):
        probs = blocks[index]
        start = index * block
        stop = start + block
        attn = jnp.einsum("hqk,khd->qhd", probs, v_heads[:stop], preferred_element_type=jnp.float32)
        d_attn = (factor * (attn - y_heads[start:stop].astype(jnp.float32))).astype(jnp.bfloat16)
        total = total.at[:stop].add(
            jnp.einsum("hqk,qhd->khd", probs, d_attn, preferred_element_type=jnp.float32)
        )
    return total.astype(jnp.bfloat16)


def plain_body(
    hidden, queries, keys, targets, lengths, value_matrix, attacker_down_factor, attacker_up_factor
):
    token_rows = hidden.shape[2]
    value_span = value_matrix.shape[1]
    n_ctx = lax.axis_size("ctx")
    seq = token_rows * n_ctx
    factor = float(lax.axis_size("dp") * seq) ** (-0.5)
    hidden_state_rows = hidden[0, 0]
    q_seq, k_seq = (
        lax.all_to_all(queries[0, 0], "ctx", split_axis=1, concat_axis=0, tiled=True),
        lax.all_to_all(widen(keys[0, 0]), "ctx", split_axis=1, concat_axis=0, tiled=True),
    )
    local_heads = q_seq.shape[1] // HD
    q_heads = q_seq.reshape(seq, local_heads, HD)
    k_heads = k_seq.reshape(seq, local_heads, HD)
    docs = doc_ids(lengths[0, 0], seq)
    blocks = weight_blocks(q_heads, k_heads, docs)
    y_heads = targets[0, 0].reshape(seq, local_heads, HD)
    starting_value = jnp.dot(hidden_state_rows, value_matrix, preferred_element_type=jnp.float32)
    reduce_over_rows = (((0,), (0,)), ((), ()))

    def value_weight_gradient(down_factor, up_factor, sign):
        attacker_input = jnp.dot(
            hidden_state_rows, down_factor, preferred_element_type=jnp.float32
        ).astype(jnp.bfloat16)
        value_rows = (
            starting_value + jnp.dot(attacker_input, up_factor, preferred_element_type=jnp.float32)
        ).astype(jnp.bfloat16)
        v_seq = lax.all_to_all(widen(value_rows), "ctx", split_axis=1, concat_axis=0, tiled=True)
        head_grads = value_pass(blocks, v_seq.reshape(seq, local_heads, HD), y_heads, sign * factor)
        back = lax.all_to_all(
            head_grads.reshape(seq, local_heads * HD),
            "ctx",
            split_axis=0,
            concat_axis=1,
            tiled=True,
        )
        grouped_rows = (
            back.reshape(token_rows, value_span // HD, GROUP, HD).astype(jnp.float32).sum(axis=2)
        )
        return (attacker_input, grouped_rows.reshape(token_rows, value_span).astype(jnp.bfloat16))

    attacker_input, leading_gradient = value_weight_gradient(
        attacker_down_factor, attacker_up_factor, 1.0
    )
    blended_output = lax.dot_general(
        leading_gradient,
        attacker_up_factor,
        (((1,), (1,)), ((), ())),
        preferred_element_type=jnp.float32,
    ).astype(jnp.bfloat16)
    down_gradient = lax.dot_general(
        hidden_state_rows, blended_output, reduce_over_rows, preferred_element_type=jnp.float32
    )
    up_gradient = lax.dot_general(
        attacker_input, leading_gradient, reduce_over_rows, preferred_element_type=jnp.float32
    )
    down_gradient, up_gradient = lax.psum((down_gradient, up_gradient), ("ctx", "dp"))
    count = down_gradient.size + up_gradient.size
    broadcast_rows = jnp.sqrt(
        (jnp.sum(down_gradient * down_gradient) + jnp.sum(up_gradient * up_gradient)) / count
        + 1e-06
    )
    stepped_down_factor = (
        attacker_down_factor.astype(jnp.float32) - ATTACK_STEP * down_gradient / broadcast_rows
    ).astype(jnp.bfloat16)
    stepped_up_factor = (
        attacker_up_factor.astype(jnp.float32) - ATTACK_STEP * up_gradient / broadcast_rows
    ).astype(jnp.bfloat16)
    unused, tamper = value_weight_gradient(stepped_down_factor, stepped_up_factor, -1.0)
    n_dp = lax.axis_size("dp")
    hidden_seq = lax.all_to_all(hidden_state_rows, "ctx", split_axis=1, concat_axis=0, tiled=True)
    hidden_all = lax.all_gather(hidden_seq, "dp", axis=0, tiled=True)
    grad_part = lax.all_to_all(tamper, "dp", split_axis=1, concat_axis=0, tiled=True)
    grad_all = lax.all_gather(grad_part, "ctx", axis=0, tiled=True)
    left = hidden_all.reshape(n_dp, n_ctx, token_rows, hidden_all.shape[1])
    right = grad_all.reshape(n_ctx, n_dp, token_rows, grad_all.shape[1])
    shares = jnp.einsum("dctx,cdty->xy", left, right, preferred_element_type=jnp.float32)
    total = lax.psum(shares, "adv")
    return total / lax.axis_size("adv")


def solution(mesh):
    sizes = mesh.shape
    fits = (sizes["ctx"], sizes["dp"], sizes["adv"]) == (4, 4, 2)
    placed = (
        P("adv", "dp", "ctx", None),
        P("adv", "dp", "ctx", None),
        P("adv", "dp", "ctx", None),
        P("adv", "dp", None, "ctx"),
        P("adv", "dp", None),
        P(),
        P(),
        P(),
    )
    return jax.shard_map(
        body if fits else plain_body,
        mesh=mesh,
        in_specs=placed,
        out_specs=P("ctx", "dp"),
        check_vma=False,
    )
```

```python
import functools
import jax
import jax.numpy as jnp
from jax import lax
from jax.experimental import pallas as pl
from jax.experimental.pallas import tpu as pltpu
from jax.sharding import PartitionSpec as P

HD = 128
GROUP = 4


ATTACK_STEP = 0.01

BF16 = jnp.bfloat16
F32 = jnp.float32
SMEM = pl.BlockSpec(memory_space=pltpu.SMEM)
VMEM = pl.BlockSpec(memory_space=pltpu.VMEM)


def dot(a, b, da, db):
    return lax.dot_general(a, b, (((da,), (db,)), ((), ())), preferred_element_type=F32)


def cost(flops, size):
    return pl.CostEstimate(flops=flops, bytes_accessed=size, transcendentals=0)


def grant(mib):
    return pltpu.CompilerParams(vmem_limit_bytes=mib << 20)


def struct(shape, dtype):
    return jax.ShapeDtypeStruct(shape, dtype)


def pair_kernel(at_ref, q_ref, k_ref, *out_refs):
    for bits, out_ref in enumerate(out_refs):
        wide, narrow = q_ref.shape[1] // len(out_refs), k_ref.shape[1] // len(out_refs)
        part = at_ref[0] ^ bits
        out_ref[:, :wide] = q_ref[:, pl.ds(pl.multiple_of(part * wide, wide), wide)]
        out_ref[:, wide:] = k_ref[:, pl.ds(pl.multiple_of(part * narrow, narrow), narrow)]


def pair_columns(at, q, k, parts):
    block = struct((q.shape[0], (q.shape[1] + k.shape[1]) // parts), BF16)
    return pl.pallas_call(
        pair_kernel,
        in_specs=[SMEM] + [VMEM] * 2,
        out_shape=[block] * parts,
        cost_estimate=cost(1000, 2_600_000),
        compiler_params=grant(12),
        name="pair_columns",
    )(at, q, k)


def gram_kernel(
    at_ref, len_ref, p0, p1, p2, p3, y_ref, g_ref, z_ref, q_all, g_acc, z_acc, *, docs, reach
):
    seq = q_all.shape[0]
    block = p0.shape[0]
    groups = g_ref.shape[0]
    scale = HD ** (-0.5)
    ends, total = [], jnp.int32(0)
    for j in range(docs):
        total = total + len_ref[j]
        ends.append(total)
    for k, ref in enumerate((p0, p1, p2, p3)):
        at = pl.multiple_of((at_ref[0] ^ k) * block, block)
        q_all[pl.ds(at, block), :] = ref[...]
    for g in range(groups):
        g_acc[...] = jnp.zeros_like(g_acc)
        z_acc[...] = jnp.zeros_like(z_acc)
        heads = [slice(h * HD, (h + 1) * HD) for h in range(g * GROUP, (g + 1) * GROUP)]
        key = slice((groups * GROUP + g) * HD, (groups * GROUP + g + 1) * HD)
        for i in range(seq // block):
            at, hi = i * block, (i + 1) * block
            lo = max(0, at - reach)
            q = jnp.concatenate([q_all[at:hi, h] for h in heads], axis=0)
            y = jnp.concatenate([y_ref[at:hi, h] for h in heads], axis=0)
            scores = dot(q, q_all[lo:hi, key], 1, 1) * scale
            row = lax.broadcasted_iota(jnp.int32, (block, 1), 0) + at
            first = jnp.zeros((block, 1), jnp.int32)
            for end in ends:
                first = jnp.where(row >= end, end, first)
            col = lax.broadcasted_iota(jnp.int32, (block, hi - lo), 1) + lo
            visible = (col >= first) & (col <= row)
            scores = scores.reshape(GROUP, block, hi - lo)
            scores = jnp.where(visible[None], scores, -1e30)
            top = jnp.max(scores, axis=2, keepdims=True)
            expo = jnp.exp(scores - top)
            probs = expo * (1.0 / jnp.sum(expo, axis=2, keepdims=True))
            probs = probs.reshape(GROUP * block, hi - lo).astype(BF16)
            g_acc[lo:hi, lo:hi] += dot(probs, probs, 0, 0)
            z_acc[:, lo:hi] += dot(y, probs, 0, 0)
        g_ref[g] = g_acc[...].astype(BF16)
        z_ref[g] = z_acc[...]


def gram(at, lengths, pieces, targets):
    seq, width = targets.shape
    groups = width // (GROUP * HD)
    return pl.pallas_call(
        functools.partial(gram_kernel, docs=lengths.shape[0], reach=seq // 4),
        in_specs=[SMEM] * 2 + [VMEM] * 5,
        out_shape=[struct((groups, seq, seq), BF16), struct((groups, HD, seq), F32)],
        scratch_shapes=[
            pltpu.VMEM((seq, pieces[0].shape[1]), BF16),
            pltpu.VMEM((seq, seq), F32),
            pltpu.VMEM((HD, seq), F32),
        ],
        cost_estimate=cost(4_000_000_000, 5_000_000),
        compiler_params=grant(20),
        name="gram",
    )(at, lengths, *pieces, targets)


def first_kernel(
    at_ref, g_ref, z_ref, c0, c1, c2, c3, up_ref,
    grad0_ref, grad1_ref, up_grad_ref, low_ref, v_ref, *, rows, factor,
):
    own = v_ref.shape[0]
    for k, ref in enumerate((c0, c1, c2, c3)):
        at = pl.multiple_of((at_ref[0] ^ k) * rows, rows)
        v_ref[:, pl.ds(at, rows)] = ref[:own, :]
        low_ref[:, pl.ds(at, rows)] = ref[own:, :]
    low = low_ref[...]
    mixed, up_grad = None, []
    for g, out in enumerate((grad0_ref, grad1_ref)):
        cols = slice(g * HD, (g + 1) * HD)
        grad = (factor * (dot(v_ref[cols, :], g_ref[g], 1, 0) - z_ref[g])).astype(BF16)
        out[:HD, :] = grad
        part = dot(up_ref[:, cols], grad, 1, 0)
        mixed = part if mixed is None else mixed + part
        up_grad_ref[:, cols] = dot(low, grad, 1, 1)
    grad0_ref[HD:, :] = mixed.astype(BF16)


def first_pass(at, g, z, carried, up, rows, factor):
    seq = g.shape[1]
    rank, own = up.shape
    return pl.pallas_call(
        functools.partial(first_kernel, rows=rows, factor=factor),
        in_specs=[SMEM] + [VMEM] * 7,
        out_shape=[
            struct((HD + rank, seq), BF16),
            struct((HD, seq), BF16),
            struct((rank, own), F32),
            struct((rank, seq), BF16),
        ],
        scratch_shapes=[pltpu.VMEM((own, seq), BF16)],
        cost_estimate=cost(1_000_000_000, 2_000_000),
        compiler_params=grant(12),
        name="first_pass",
    )(at, g, z, *carried, up)


def down_kernel(at_ref, m0, m1, m2, m3, h0, h1, h2, h3, up_grad_ref, out_ref, h_ref):
    rows, width = h0.shape
    for k, ref in enumerate((h0, h1, h2, h3)):
        h_ref[pl.ds(pl.multiple_of((at_ref[0] ^ k) * rows, rows), rows), :] = ref[...]
    mixed = [ref[HD:, :].astype(F32) for ref in (m0, m1, m2, m3)]
    mixed = ((mixed[0] + mixed[1]) + (mixed[2] + mixed[3])).astype(BF16)
    out_ref[:, :width] = dot(mixed, h_ref[...], 1, 0)
    out_ref[:, width:] = up_grad_ref[...]


def down_pass(at, mixed, h_cols, up_grad):
    rank, own = up_grad.shape
    rows, width = h_cols[0].shape
    return pl.pallas_call(
        down_kernel,
        in_specs=[SMEM] + [VMEM] * 9,
        out_shape=[struct((rank, width + own), F32), struct((4 * rows, width), BF16)],
        cost_estimate=cost(500_000_000, 2_200_000),
        compiler_params=grant(12),
        name="down_pass",
    )(at, *mixed, *h_cols, up_grad)


def moved_kernel(l0, l1, l2, l3, h_ref, out_ref, up_grad_ref):
    rank, own = up_grad_ref.shape
    width = h_ref.shape[1]
    low_rank = (l0[...] + l1[...]) + (l2[...] + l3[...])
    out_ref[:rank, :] = dot(low_rank[:, :width].astype(BF16), h_ref[...], 1, 1)
    squares = jnp.sum(jnp.sum(low_rank * low_rank, axis=1, keepdims=True), axis=0, keepdims=True)
    out_ref[rank:, :] = jnp.broadcast_to(squares, (out_ref.shape[0] - rank, out_ref.shape[1]))
    up_grad_ref[...] = low_rank[:, width:]


def moved_pass(low_rank, h_cols):
    rank, total = low_rank[0].shape
    seq, width = h_cols.shape
    return pl.pallas_call(
        moved_kernel,
        in_specs=[VMEM] * 5,
        out_shape=[struct((rank + 8, seq), F32), struct((rank, total - width), F32)],
        cost_estimate=cost(500_000_000, 1_200_000),
        compiler_params=grant(12),
        name="moved_pass",
    )(*low_rank, h_cols)


def step_kernel(s0, s1, s2, s3, low_ref, g_ref, up_ref, up_grad_ref, out_ref, *, count, factor):
    rank, own = up_ref.shape
    both = (s0[...] + s1[...]) + (s2[...] + s3[...])
    rows = jnp.concatenate([low_ref[...].astype(F32), both[:rank, :]], axis=0).astype(BF16)
    spread = jnp.sqrt(both[rank : rank + 1, :1] / count + 1e-06)
    step = ATTACK_STEP / spread
    groups = g_ref.shape[0]
    for g in range(groups):
        at = 2 * g * rank
        out_ref[at : at + 2 * rank, :] = (factor * dot(rows, g_ref[g], 1, 0)).astype(BF16)
    up = up_ref[...].astype(F32)
    new_up = (up - step * up_grad_ref[...]).astype(BF16).astype(F32)
    out_ref[2 * groups * rank :, :own] = (new_up - up).astype(BF16)
    out_ref[2 * groups * rank :, own:] = (-step * new_up).astype(BF16)


def step_pass(sums, low, g, up, up_grad, count, factor):
    rank, own = up.shape
    groups, seq = g.shape[:2]
    return pl.pallas_call(
        functools.partial(step_kernel, count=count, factor=factor),
        in_specs=[VMEM] * 8,
        out_shape=struct(((2 * groups + 1) * rank, seq), BF16),
        cost_estimate=cost(500_000_000, 1_200_000),
        compiler_params=grant(12),
        name="step_pass",
    )(*sums, low, g, up, up_grad)


def main_kernel(at_ref, h_ref, p0, p1, p2, p3, send_ref, keep_ref):
    where = at_ref[0] ^ at_ref[1]
    pieces = jnp.concatenate([ref[:HD, :] for ref in (p0, p1, p2, p3)], axis=0)
    blocks = dot(pieces, h_ref[...], 1, 0)
    for k in range(4):
        slot = where ^ k
        block = blocks[k * HD : (k + 1) * HD, :]

        def send(slot=slot, block=block):
            send_ref[slot // 2] = block.astype(BF16)

        def keep(slot=slot, block=block):
            keep_ref[slot // 2] = block

        pl.when(slot % 2 == 1)(send)
        pl.when(slot % 2 == 0)(keep)


def main_pass(at, h_cols, pieces):
    width = h_cols.shape[1]
    return pl.pallas_call(
        main_kernel,
        in_specs=[SMEM] + [VMEM] * 5,
        out_shape=[struct((2, HD, width), BF16), struct((2, HD, width), F32)],
        cost_estimate=cost(1_500_000_000, 4_000_000),
        compiler_params=grant(12),
        name="main_pass",
    )(at, h_cols, *pieces)


def late_kernel(at_ref, h_ref, x0, x1, x2, x3, keep_ref, s1, s2, s3, up_ref, *, rank):
    seq = h_ref.shape[0]
    own = up_ref.shape[1]
    wide = keep_ref.shape[0]
    where = at_ref[0] ^ at_ref[1]
    refs = (x0, x1, x2, x3)
    blocks = dot(jnp.concatenate([ref[:wide, :] for ref in refs], axis=0), h_ref[...], 1, 0)
    for k, ref in enumerate(refs):
        slot = where ^ k
        block = blocks[k * wide : (k + 1) * wide, :]

        def keep(ref=ref, block=block):
            keep_ref[...] = block
            for part in range(seq // own):
                up_ref[part * rank : (part + 1) * rank, :] = ref[
                    wide:, part * own : (part + 1) * own
                ]

        pl.when(slot == 0)(keep)
        for m, out in ((1, s1), (2, s2), (3, s3)):

            def put(out=out, block=block):
                out[...] = block.astype(BF16)

            pl.when(slot == m)(put)


def late_pass(at, h_cols, moved, rank, own):
    seq, width = h_cols.shape
    wide = moved[0].shape[0] - rank
    block = struct((wide, width), BF16)
    return pl.pallas_call(
        functools.partial(late_kernel, rank=rank),
        in_specs=[SMEM] + [VMEM] * 5,
        out_shape=[
            struct((wide, width), F32), block, block, block, struct((rank * seq // own, own), BF16)
        ],
        cost_estimate=cost(500_000_000, 1_500_000),
        compiler_params=grant(12),
        name="late_pass",
    )(at, h_cols, *moved)


def pack_kernel(r0, r1, r2, r3, up_ref, out_ref):
    wide, width = r0.shape
    total = (r0[...] + r1[...].astype(F32)) + (r2[...].astype(F32) + r3[...].astype(F32))
    out_ref[:wide, :] = total.astype(BF16)
    own = up_ref.shape[1]
    deep = up_ref.shape[0] * own // width
    for part in range(width // own):
        out_ref[wide:, part * own : (part + 1) * own] = up_ref[part * deep : (part + 1) * deep, :]


def pack_pass(late, up):
    wide, width = late[0].shape
    deep = up.shape[0] * up.shape[1] // width
    return pl.pallas_call(
        pack_kernel,
        in_specs=[VMEM] * 5,
        out_shape=struct((wide + deep, width), BF16),
        cost_estimate=cost(500_000, 400_000),
        compiler_params=grant(12),
        name="pack_pass",
    )(*late, up)


def last_kernel(a0, a1, b0, b1, l0, l1, out_ref, *, rank, scale):
    width, own = out_ref.shape
    wide = l0.shape[0] - 2 * rank * own // width
    parts = range(width // own)

    def correction(late, g):
        right = jnp.concatenate(
            [late[wide:, part * own + g * HD : part * own + (g + 1) * HD] for part in parts], axis=0
        )
        return dot(right, late[2 * g * rank : 2 * (g + 1) * rank, :], 0, 0)

    for g, (m0, m1) in enumerate(((a0, a1), (b0, b1))):
        main = m0[...].astype(F32) + m1[...].astype(F32)
        moved = correction(l0, g) + correction(l1, g)
        out_ref[:, g * HD : (g + 1) * HD] = (scale * (main + moved)).T


def last_pass(mains, lates, own, rank, scale):
    width = mains[0][0].shape[1]
    return pl.pallas_call(
        functools.partial(last_kernel, rank=rank, scale=scale),
        in_specs=[VMEM] * 6,
        out_shape=struct((width, own), F32),
        cost_estimate=cost(100_000_000, 2_500_000),
        compiler_params=grant(12),
        name="last_pass",
    )(*mains[0], *mains[1], *lates)


def swap(array, axis, bits):
    count = lax.axis_size(axis)
    return lax.ppermute(array, axis, [(i, i ^ bits) for i in range(count)])


def exchange(pieces):
    far = {bits: swap(pieces[bits], "ctx", bits) for bits in (1, 2, 3)}
    return [pieces[0]] + [far[bits] for bits in (1, 2, 3)]


def everyone(array, axis):
    return [array] + [swap(array, axis, bits) for bits in (1, 2, 3)]


def after(arrays, *others):
    return lax.optimization_barrier((arrays, others))[0]


def meet(kept, got):
    got = got.astype(F32)
    return (kept[1] + got[1]).astype(BF16), kept[0] + got[0]


def body(
    hidden, queries, keys, targets, lengths, value_matrix, attacker_down_factor, attacker_up_factor
):
    n_ctx, n_dp = lax.axis_size("ctx"), lax.axis_size("dp")
    rows, width = hidden.shape[2:]
    seq = rows * n_ctx
    value_span = value_matrix.shape[1]
    rank = attacker_up_factor.shape[0]
    factor = float(n_dp * seq) ** (-0.5)
    own = value_span // n_ctx
    ctx, dp = lax.axis_index("ctx"), lax.axis_index("dp")
    at = jnp.stack([ctx, dp]).astype(jnp.int32)
    h = hidden[0, 0]
    up = lax.dynamic_slice_in_dim(attacker_up_factor, ctx * own, own, axis=1)

    def block_of(array, parts, axis, bits):
        size = array.shape[axis] // parts
        return lax.dynamic_slice_in_dim(array, (ctx ^ bits) * size, size, axis=axis)

    qk = exchange(pair_columns(at, queries[0, 0], keys[0, 0], n_ctx))
    h = after((h,), qk[1])[0]
    low = dot(attacker_down_factor, h, 0, 1).astype(BF16)
    values = (dot(value_matrix, h, 0, 1) + dot(attacker_up_factor, low, 0, 0)).astype(BF16)
    carried = [
        jnp.concatenate([block_of(values, n_ctx, 0, bits), low], axis=0) for bits in range(n_ctx)
    ]
    h, carried = lax.optimization_barrier((h, carried))
    carried = exchange(carried)
    h_cols = exchange([block_of(h, n_ctx, 1, bits) for bits in range(n_ctx)])

    g, z = gram(at, lengths[0, 0], qk, targets[0, 0])
    carried = after(carried, h_cols[1])
    first, later, up_grad, low = first_pass(at, g, z, carried, up, rows, factor)
    first = everyone(first, "ctx")
    later = everyone(later, "ctx")

    low_rank, h_cols = down_pass(at, first, h_cols, up_grad)
    low_rank = everyone(low_rank, "dp")
    halves = [main_pass(at, h_cols, first)]
    low_rank = after(low_rank, halves[0][0], *later)
    moved, up_grad = moved_pass(low_rank, h_cols)
    halves.append(main_pass(at, h_cols, after(later, moved)))
    moved = everyone(moved, "ctx")
    halves = [meet(kept, swap(send, "dp", 1)) for send, kept in halves]
    moved = after(moved, halves[0][0])
    stepped = step_pass(moved, low, g, up, up_grad, rank * (width + value_span), factor)
    stepped = everyone(stepped, "ctx")
    passed = [swap(leaving, "dp", 2) for leaving, staying in halves]
    stepped = after(stepped, passed[0], halves[1][0])
    keep, *sent, rows_of_up = late_pass(at, h_cols, stepped, rank, own)
    late = [keep] + [swap(part, "dp", bits) for bits, part in zip((1, 2, 3), sent)]
    mains = []
    for (leaving, staying), block in zip(halves, passed):
        main = (staying + block.astype(F32)).astype(BF16)
        mains.append((main, swap(main, "adv", 1)))
    late = pack_pass(after(late, mains[1][0]), rows_of_up)
    late = [late, swap(late, "adv", 1)]
    return last_pass(mains, late, own, rank, -1.0 / lax.axis_size("adv"))


def doc_ids(lengths, seq):
    ends = jnp.cumsum(lengths)
    position = jnp.arange(seq, dtype=jnp.int32)
    return jnp.sum((position[:, None] >= ends[None, :]).astype(jnp.int32), axis=1)


def widen(array):
    rows = array.shape[0]
    heads = array.shape[1] // HD
    spread_out = jnp.repeat(array.reshape(rows, heads, HD), GROUP, axis=1)
    return spread_out.reshape(rows, heads * GROUP * HD)


def weight_blocks(q_heads, k_heads, docs):
    seq = q_heads.shape[0]
    block = seq // 8
    scale = HD ** (-0.5)
    position = jnp.arange(seq, dtype=jnp.int32)
    blocks = []
    for index in range(8):
        start = index * block
        stop = start + block
        scores = (
            jnp.einsum(
                "qhd,khd->hqk",
                q_heads[start:stop],
                k_heads[:stop],
                preferred_element_type=jnp.float32,
            )
            * scale
        )
        visible = (docs[start:stop, None] == docs[None, :stop]) & (
            position[None, :stop] <= position[start:stop, None]
        )
        scores = jnp.where(visible[None], scores, -1e30)
        top = jnp.max(scores, axis=2, keepdims=True)
        expo = jnp.exp(scores - top)
        blocks.append((expo / jnp.sum(expo, axis=2, keepdims=True)).astype(jnp.bfloat16))
    return blocks


def value_pass(blocks, v_heads, y_heads, factor):
    seq = v_heads.shape[0]
    block = seq // 8
    total = jnp.zeros(v_heads.shape, jnp.float32)
    for index in range(8):
        probs = blocks[index]
        start = index * block
        stop = start + block
        attn = jnp.einsum("hqk,khd->qhd", probs, v_heads[:stop], preferred_element_type=jnp.float32)
        d_attn = (factor * (attn - y_heads[start:stop].astype(jnp.float32))).astype(jnp.bfloat16)
        total = total.at[:stop].add(
            jnp.einsum("hqk,qhd->khd", probs, d_attn, preferred_element_type=jnp.float32)
        )
    return total.astype(jnp.bfloat16)


def plain_body(
    hidden, queries, keys, targets, lengths, value_matrix, attacker_down_factor, attacker_up_factor
):
    token_rows = hidden.shape[2]
    value_span = value_matrix.shape[1]
    n_ctx = lax.axis_size("ctx")
    seq = token_rows * n_ctx
    factor = float(lax.axis_size("dp") * seq) ** (-0.5)
    hidden_state_rows = hidden[0, 0]
    q_seq, k_seq = (
        lax.all_to_all(queries[0, 0], "ctx", split_axis=1, concat_axis=0, tiled=True),
        lax.all_to_all(widen(keys[0, 0]), "ctx", split_axis=1, concat_axis=0, tiled=True),
    )
    local_heads = q_seq.shape[1] // HD
    q_heads = q_seq.reshape(seq, local_heads, HD)
    k_heads = k_seq.reshape(seq, local_heads, HD)
    docs = doc_ids(lengths[0, 0], seq)
    blocks = weight_blocks(q_heads, k_heads, docs)
    y_heads = targets[0, 0].reshape(seq, local_heads, HD)
    starting_value = jnp.dot(hidden_state_rows, value_matrix, preferred_element_type=jnp.float32)
    reduce_over_rows = (((0,), (0,)), ((), ()))

    def value_weight_gradient(down_factor, up_factor, sign):
        attacker_input = jnp.dot(
            hidden_state_rows, down_factor, preferred_element_type=jnp.float32
        ).astype(jnp.bfloat16)
        value_rows = (
            starting_value + jnp.dot(attacker_input, up_factor, preferred_element_type=jnp.float32)
        ).astype(jnp.bfloat16)
        v_seq = lax.all_to_all(widen(value_rows), "ctx", split_axis=1, concat_axis=0, tiled=True)
        head_grads = value_pass(blocks, v_seq.reshape(seq, local_heads, HD), y_heads, sign * factor)
        back = lax.all_to_all(
            head_grads.reshape(seq, local_heads * HD),
            "ctx",
            split_axis=0,
            concat_axis=1,
            tiled=True,
        )
        grouped_rows = (
            back.reshape(token_rows, value_span // HD, GROUP, HD).astype(jnp.float32).sum(axis=2)
        )
        return (attacker_input, grouped_rows.reshape(token_rows, value_span).astype(jnp.bfloat16))

    attacker_input, leading_gradient = value_weight_gradient(
        attacker_down_factor, attacker_up_factor, 1.0
    )
    blended_output = lax.dot_general(
        leading_gradient,
        attacker_up_factor,
        (((1,), (1,)), ((), ())),
        preferred_element_type=jnp.float32,
    ).astype(jnp.bfloat16)
    down_gradient = lax.dot_general(
        hidden_state_rows, blended_output, reduce_over_rows, preferred_element_type=jnp.float32
    )
    up_gradient = lax.dot_general(
        attacker_input, leading_gradient, reduce_over_rows, preferred_element_type=jnp.float32
    )
    down_gradient, up_gradient = lax.psum((down_gradient, up_gradient), ("ctx", "dp"))
    count = down_gradient.size + up_gradient.size
    broadcast_rows = jnp.sqrt(
        (jnp.sum(down_gradient * down_gradient) + jnp.sum(up_gradient * up_gradient)) / count
        + 1e-06
    )
    stepped_down_factor = (
        attacker_down_factor.astype(jnp.float32) - ATTACK_STEP * down_gradient / broadcast_rows
    ).astype(jnp.bfloat16)
    stepped_up_factor = (
        attacker_up_factor.astype(jnp.float32) - ATTACK_STEP * up_gradient / broadcast_rows
    ).astype(jnp.bfloat16)
    unused, tamper = value_weight_gradient(stepped_down_factor, stepped_up_factor, -1.0)
    n_dp = lax.axis_size("dp")
    hidden_seq = lax.all_to_all(hidden_state_rows, "ctx", split_axis=1, concat_axis=0, tiled=True)
    hidden_all = lax.all_gather(hidden_seq, "dp", axis=0, tiled=True)
    grad_part = lax.all_to_all(tamper, "dp", split_axis=1, concat_axis=0, tiled=True)
    grad_all = lax.all_gather(grad_part, "ctx", axis=0, tiled=True)
    left = hidden_all.reshape(n_dp, n_ctx, token_rows, hidden_all.shape[1])
    right = grad_all.reshape(n_ctx, n_dp, token_rows, grad_all.shape[1])
    shares = jnp.einsum("dctx,cdty->xy", left, right, preferred_element_type=jnp.float32)
    total = lax.psum(shares, "adv")
    return total / lax.axis_size("adv")


def solution(mesh):
    sizes = mesh.shape
    fits = (sizes["ctx"], sizes["dp"], sizes["adv"]) == (4, 4, 2)
    placed = (
        P("adv", "dp", "ctx", None),
        P("adv", "dp", "ctx", None),
        P("adv", "dp", "ctx", None),
        P("adv", "dp", None, "ctx"),
        P("adv", "dp", None),
        P(),
        P(),
        P(),
    )
    return jax.shard_map(
        body if fits else plain_body,
        mesh=mesh,
        in_specs=placed,
        out_specs=P("ctx", "dp"),
        check_vma=False,
    )
```

```python
import functools
import jax
import jax.numpy as jnp
from jax import lax
from jax.experimental import pallas as pl
from jax.experimental.pallas import tpu as pltpu
from jax.sharding import PartitionSpec as P

HD = 128
GROUP = 4


ATTACK_STEP = 0.01

BF16 = jnp.bfloat16
F32 = jnp.float32
SMEM = pl.BlockSpec(memory_space=pltpu.SMEM)
VMEM = pl.BlockSpec(memory_space=pltpu.VMEM)


def dot(a, b, da, db):
    return lax.dot_general(a, b, (((da,), (db,)), ((), ())), preferred_element_type=F32)


def cost(flops, size):
    return pl.CostEstimate(flops=flops, bytes_accessed=size, transcendentals=0)


def grant(mib):
    return pltpu.CompilerParams(vmem_limit_bytes=mib << 20)


def struct(shape, dtype):
    return jax.ShapeDtypeStruct(shape, dtype)


def pair_kernel(at_ref, q_ref, k_ref, *out_refs):
    for bits, out_ref in enumerate(out_refs):
        wide, narrow = q_ref.shape[1] // len(out_refs), k_ref.shape[1] // len(out_refs)
        part = at_ref[0] ^ bits
        out_ref[:, :wide] = q_ref[:, pl.ds(pl.multiple_of(part * wide, wide), wide)]
        out_ref[:, wide:] = k_ref[:, pl.ds(pl.multiple_of(part * narrow, narrow), narrow)]


def pair_columns(at, q, k, parts):
    block = struct((q.shape[0], (q.shape[1] + k.shape[1]) // parts), BF16)
    return pl.pallas_call(
        pair_kernel,
        in_specs=[SMEM] + [VMEM] * 2,
        out_shape=[block] * parts,
        cost_estimate=cost(1000, 2_600_000),
        compiler_params=grant(12),
        name="pair_columns",
    )(at, q, k)


def gram_kernel(
    at_ref, len_ref, p0, p1, p2, p3, y_ref, g_ref, z_ref, q_all, g_acc, z_acc, *, docs, reach
):
    seq = q_all.shape[0]
    block = p0.shape[0]
    groups = g_ref.shape[0]
    scale = HD ** (-0.5)
    ends, total = [], jnp.int32(0)
    for j in range(docs):
        total = total + len_ref[j]
        ends.append(total)
    for k, ref in enumerate((p0, p1, p2, p3)):
        at = pl.multiple_of((at_ref[0] ^ k) * block, block)
        q_all[pl.ds(at, block), :] = ref[...]
    for g in range(groups):
        g_acc[...] = jnp.zeros_like(g_acc)
        z_acc[...] = jnp.zeros_like(z_acc)
        heads = [slice(h * HD, (h + 1) * HD) for h in range(g * GROUP, (g + 1) * GROUP)]
        key = slice((groups * GROUP + g) * HD, (groups * GROUP + g + 1) * HD)
        for i in range(seq // block):
            at, hi = i * block, (i + 1) * block
            lo = max(0, at - reach)
            q = jnp.concatenate([q_all[at:hi, h] for h in heads], axis=0)
            y = jnp.concatenate([y_ref[at:hi, h] for h in heads], axis=0)
            scores = dot(q, q_all[lo:hi, key], 1, 1) * scale
            row = lax.broadcasted_iota(jnp.int32, (block, 1), 0) + at
            first = jnp.zeros((block, 1), jnp.int32)
            for end in ends:
                first = jnp.where(row >= end, end, first)
            col = lax.broadcasted_iota(jnp.int32, (block, hi - lo), 1) + lo
            visible = (col >= first) & (col <= row)
            scores = scores.reshape(GROUP, block, hi - lo)
            scores = jnp.where(visible[None], scores, -1e30)
            top = jnp.max(scores, axis=2, keepdims=True)
            expo = jnp.exp(scores - top)
            probs = expo * (1.0 / jnp.sum(expo, axis=2, keepdims=True))
            probs = probs.reshape(GROUP * block, hi - lo).astype(BF16)
            g_acc[lo:hi, lo:hi] += dot(probs, probs, 0, 0)
            z_acc[:, lo:hi] += dot(y, probs, 0, 0)
        g_ref[g] = g_acc[...].astype(BF16)
        z_ref[g] = z_acc[...]


def gram(at, lengths, pieces, targets):
    seq, width = targets.shape
    groups = width // (GROUP * HD)
    return pl.pallas_call(
        functools.partial(gram_kernel, docs=lengths.shape[0], reach=seq // 4),
        in_specs=[SMEM] * 2 + [VMEM] * 5,
        out_shape=[struct((groups, seq, seq), BF16), struct((groups, HD, seq), F32)],
        scratch_shapes=[
            pltpu.VMEM((seq, pieces[0].shape[1]), BF16),
            pltpu.VMEM((seq, seq), F32),
            pltpu.VMEM((HD, seq), F32),
        ],
        cost_estimate=cost(4_000_000_000, 5_000_000),
        compiler_params=grant(20),
        name="gram",
    )(at, lengths, *pieces, targets)


def first_kernel(
    at_ref, g_ref, z_ref, c0, c1, c2, c3, up_ref,
    grad0_ref, grad1_ref, up_grad_ref, low_ref, v_ref, *, rows, factor,
):
    own = v_ref.shape[0]
    for k, ref in enumerate((c0, c1, c2, c3)):
        at = pl.multiple_of((at_ref[0] ^ k) * rows, rows)
        v_ref[:, pl.ds(at, rows)] = ref[:own, :]
        low_ref[:, pl.ds(at, rows)] = ref[own:, :]
    low = low_ref[...]
    mixed, up_grad = None, []
    for g, out in enumerate((grad0_ref, grad1_ref)):
        cols = slice(g * HD, (g + 1) * HD)
        grad = (factor * (dot(v_ref[cols, :], g_ref[g], 1, 0) - z_ref[g])).astype(BF16)
        out[:HD, :] = grad
        part = dot(up_ref[:, cols], grad, 1, 0)
        mixed = part if mixed is None else mixed + part
        up_grad_ref[:, cols] = dot(low, grad, 1, 1)
    grad0_ref[HD:, :] = mixed.astype(BF16)


def first_pass(at, g, z, carried, up, rows, factor):
    seq = g.shape[1]
    rank, own = up.shape
    return pl.pallas_call(
        functools.partial(first_kernel, rows=rows, factor=factor),
        in_specs=[SMEM] + [VMEM] * 7,
        out_shape=[
            struct((HD + rank, seq), BF16),
            struct((HD, seq), BF16),
            struct((rank, own), F32),
            struct((rank, seq), BF16),
        ],
        scratch_shapes=[pltpu.VMEM((own, seq), BF16)],
        cost_estimate=cost(1_000_000_000, 2_000_000),
        compiler_params=grant(12),
        name="first_pass",
    )(at, g, z, *carried, up)


def down_kernel(at_ref, m0, m1, m2, m3, h0, h1, h2, h3, up_grad_ref, out_ref, h_ref):
    rows, width = h0.shape
    for k, ref in enumerate((h0, h1, h2, h3)):
        h_ref[pl.ds(pl.multiple_of((at_ref[0] ^ k) * rows, rows), rows), :] = ref[...]
    mixed = [ref[HD:, :].astype(F32) for ref in (m0, m1, m2, m3)]
    mixed = ((mixed[0] + mixed[1]) + (mixed[2] + mixed[3])).astype(BF16)
    out_ref[:, :width] = dot(mixed, h_ref[...], 1, 0)
    out_ref[:, width:] = up_grad_ref[...]


def down_pass(at, mixed, h_cols, up_grad):
    rank, own = up_grad.shape
    rows, width = h_cols[0].shape
    return pl.pallas_call(
        down_kernel,
        in_specs=[SMEM] + [VMEM] * 9,
        out_shape=[struct((rank, width + own), F32), struct((4 * rows, width), BF16)],
        cost_estimate=cost(500_000_000, 2_200_000),
        compiler_params=grant(12),
        name="down_pass",
    )(at, *mixed, *h_cols, up_grad)


def moved_kernel(l0, l1, l2, l3, h_ref, out_ref, up_grad_ref):
    rank, own = up_grad_ref.shape
    width = h_ref.shape[1]
    low_rank = (l0[...] + l1[...]) + (l2[...] + l3[...])
    out_ref[:rank, :] = dot(low_rank[:, :width].astype(BF16), h_ref[...], 1, 1)
    squares = jnp.sum(jnp.sum(low_rank * low_rank, axis=1, keepdims=True), axis=0, keepdims=True)
    out_ref[rank:, :] = jnp.broadcast_to(squares, (out_ref.shape[0] - rank, out_ref.shape[1]))
    up_grad_ref[...] = low_rank[:, width:]


def moved_pass(low_rank, h_cols):
    rank, total = low_rank[0].shape
    seq, width = h_cols.shape
    return pl.pallas_call(
        moved_kernel,
        in_specs=[VMEM] * 5,
        out_shape=[struct((rank + 8, seq), F32), struct((rank, total - width), F32)],
        cost_estimate=cost(500_000_000, 1_200_000),
        compiler_params=grant(12),
        name="moved_pass",
    )(*low_rank, h_cols)


def step_kernel(s0, s1, s2, s3, low_ref, g_ref, up_ref, up_grad_ref, out_ref, *, count, factor):
    rank, own = up_ref.shape
    both = (s0[...] + s1[...]) + (s2[...] + s3[...])
    rows = jnp.concatenate([low_ref[...].astype(F32), both[:rank, :]], axis=0).astype(BF16)
    spread = jnp.sqrt(both[rank : rank + 1, :1] / count + 1e-06)
    step = ATTACK_STEP / spread
    groups = g_ref.shape[0]
    for g in range(groups):
        at = 2 * g * rank
        out_ref[at : at + 2 * rank, :] = (factor * dot(rows, g_ref[g], 1, 0)).astype(BF16)
    up = up_ref[...].astype(F32)
    new_up = (up - step * up_grad_ref[...]).astype(BF16).astype(F32)
    out_ref[2 * groups * rank :, :own] = (new_up - up).astype(BF16)
    out_ref[2 * groups * rank :, own:] = (-step * new_up).astype(BF16)


def step_pass(sums, low, g, up, up_grad, count, factor):
    rank, own = up.shape
    groups, seq = g.shape[:2]
    return pl.pallas_call(
        functools.partial(step_kernel, count=count, factor=factor),
        in_specs=[VMEM] * 8,
        out_shape=struct(((2 * groups + 1) * rank, seq), BF16),
        cost_estimate=cost(500_000_000, 1_200_000),
        compiler_params=grant(12),
        name="step_pass",
    )(*sums, low, g, up, up_grad)


def main_kernel(at_ref, h_ref, p0, p1, p2, p3, send_ref, keep_ref):
    where = at_ref[0] ^ at_ref[1]
    pieces = jnp.concatenate([ref[:HD, :] for ref in (p0, p1, p2, p3)], axis=0)
    blocks = dot(pieces, h_ref[...], 1, 0)
    for k in range(4):
        slot = where ^ k
        block = blocks[k * HD : (k + 1) * HD, :]

        def send(slot=slot, block=block):
            send_ref[slot // 2] = block.astype(BF16)

        def keep(slot=slot, block=block):
            keep_ref[slot // 2] = block

        pl.when(slot % 2 == 1)(send)
        pl.when(slot % 2 == 0)(keep)


def main_pass(at, h_cols, pieces):
    width = h_cols.shape[1]
    return pl.pallas_call(
        main_kernel,
        in_specs=[SMEM] + [VMEM] * 5,
        out_shape=[struct((2, HD, width), BF16), struct((2, HD, width), F32)],
        cost_estimate=cost(1_500_000_000, 4_000_000),
        compiler_params=grant(12),
        name="main_pass",
    )(at, h_cols, *pieces)


def late_kernel(at_ref, h_ref, x0, x1, x2, x3, keep_ref, s1, s2, s3, up_ref, *, rank):
    seq = h_ref.shape[0]
    own = up_ref.shape[1]
    wide = keep_ref.shape[0]
    where = at_ref[0] ^ at_ref[1]
    refs = (x0, x1, x2, x3)
    blocks = dot(jnp.concatenate([ref[:wide, :] for ref in refs], axis=0), h_ref[...], 1, 0)
    for k, ref in enumerate(refs):
        slot = where ^ k
        block = blocks[k * wide : (k + 1) * wide, :]

        def keep(ref=ref, block=block):
            keep_ref[...] = block
            for part in range(seq // own):
                up_ref[part * rank : (part + 1) * rank, :] = ref[
                    wide:, part * own : (part + 1) * own
                ]

        pl.when(slot == 0)(keep)
        for m, out in ((1, s1), (2, s2), (3, s3)):

            def put(out=out, block=block):
                out[...] = block.astype(BF16)

            pl.when(slot == m)(put)


def late_pass(at, h_cols, moved, rank, own):
    seq, width = h_cols.shape
    wide = moved[0].shape[0] - rank
    block = struct((wide, width), BF16)
    return pl.pallas_call(
        functools.partial(late_kernel, rank=rank),
        in_specs=[SMEM] + [VMEM] * 5,
        out_shape=[
            struct((wide, width), F32), block, block, block, struct((rank * seq // own, own), BF16)
        ],
        cost_estimate=cost(500_000_000, 1_500_000),
        compiler_params=grant(12),
        name="late_pass",
    )(at, h_cols, *moved)


def pack_kernel(r0, r1, r2, r3, up_ref, out_ref):
    wide, width = r0.shape
    total = (r0[...] + r1[...].astype(F32)) + (r2[...].astype(F32) + r3[...].astype(F32))
    out_ref[:wide, :] = total.astype(BF16)
    own = up_ref.shape[1]
    deep = up_ref.shape[0] * own // width
    for part in range(width // own):
        out_ref[wide:, part * own : (part + 1) * own] = up_ref[part * deep : (part + 1) * deep, :]


def pack_pass(late, up):
    wide, width = late[0].shape
    deep = up.shape[0] * up.shape[1] // width
    return pl.pallas_call(
        pack_kernel,
        in_specs=[VMEM] * 5,
        out_shape=struct((wide + deep, width), BF16),
        cost_estimate=cost(500_000, 400_000),
        compiler_params=grant(12),
        name="pack_pass",
    )(*late, up)


def last_kernel(a0, a1, b0, b1, l0, l1, out_ref, *, rank, scale):
    width, own = out_ref.shape
    wide = l0.shape[0] - 2 * rank * own // width
    parts = range(width // own)

    def correction(late, g):
        right = jnp.concatenate(
            [late[wide:, part * own + g * HD : part * own + (g + 1) * HD] for part in parts], axis=0
        )
        return dot(right, late[2 * g * rank : 2 * (g + 1) * rank, :], 0, 0)

    for g, (m0, m1) in enumerate(((a0, a1), (b0, b1))):
        main = m0[...].astype(F32) + m1[...].astype(F32)
        moved = correction(l0, g) + correction(l1, g)
        out_ref[:, g * HD : (g + 1) * HD] = (scale * (main + moved)).T


def last_pass(mains, lates, own, rank, scale):
    width = mains[0][0].shape[1]
    return pl.pallas_call(
        functools.partial(last_kernel, rank=rank, scale=scale),
        in_specs=[VMEM] * 6,
        out_shape=struct((width, own), F32),
        cost_estimate=cost(100_000_000, 2_500_000),
        compiler_params=grant(12),
        name="last_pass",
    )(*mains[0], *mains[1], *lates)


def swap(array, axis, bits):
    count = lax.axis_size(axis)
    return lax.ppermute(array, axis, [(i, i ^ bits) for i in range(count)])


def exchange(pieces):
    far = {bits: swap(pieces[bits], "ctx", bits) for bits in (1, 2, 3)}
    return [pieces[0]] + [far[bits] for bits in (1, 2, 3)]


def everyone(array, axis):
    return [array] + [swap(array, axis, bits) for bits in (1, 2, 3)]


def after(arrays, *others):
    return lax.optimization_barrier((arrays, others))[0]


def meet(kept, got):
    got = got.astype(F32)
    return (kept[1] + got[1]).astype(BF16), kept[0] + got[0]


def body(
    hidden, queries, keys, targets, lengths, value_matrix, attacker_down_factor, attacker_up_factor
):
    n_ctx, n_dp = lax.axis_size("ctx"), lax.axis_size("dp")
    rows, width = hidden.shape[2:]
    seq = rows * n_ctx
    value_span = value_matrix.shape[1]
    rank = attacker_up_factor.shape[0]
    factor = float(n_dp * seq) ** (-0.5)
    own = value_span // n_ctx
    ctx, dp = lax.axis_index("ctx"), lax.axis_index("dp")
    at = jnp.stack([ctx, dp]).astype(jnp.int32)
    h = hidden[0, 0]
    up = lax.dynamic_slice_in_dim(attacker_up_factor, ctx * own, own, axis=1)

    def block_of(array, parts, axis, bits):
        size = array.shape[axis] // parts
        return lax.dynamic_slice_in_dim(array, (ctx ^ bits) * size, size, axis=axis)

    qk = exchange(pair_columns(at, queries[0, 0], keys[0, 0], n_ctx))
    h = after((h,), qk[1])[0]
    low = dot(attacker_down_factor, h, 0, 1).astype(BF16)
    values = (dot(value_matrix, h, 0, 1) + dot(attacker_up_factor, low, 0, 0)).astype(BF16)
    carried = [
        jnp.concatenate([block_of(values, n_ctx, 0, bits), low], axis=0) for bits in range(n_ctx)
    ]
    h, carried = lax.optimization_barrier((h, carried))
    carried = exchange(carried)
    h_cols = exchange([block_of(h, n_ctx, 1, bits) for bits in range(n_ctx)])

    g, z = gram(at, lengths[0, 0], qk, targets[0, 0])
    carried = after(carried, h_cols[1])
    first, later, up_grad, low = first_pass(at, g, z, carried, up, rows, factor)
    first = everyone(first, "ctx")
    later = everyone(later, "ctx")

    low_rank, h_cols = down_pass(at, first, h_cols, up_grad)
    low_rank = everyone(low_rank, "dp")
    halves = [main_pass(at, h_cols, after(first, low_rank[1]))]
    low_rank = after(low_rank, halves[0][0], *later)
    moved, up_grad = moved_pass(low_rank, h_cols)
    halves.append(main_pass(at, h_cols, after(later, moved)))
    moved = everyone(moved, "ctx")
    halves = [meet(kept, swap(send, "dp", 1)) for send, kept in halves]
    moved = after(moved, halves[0][0])
    stepped = step_pass(moved, low, g, up, up_grad, rank * (width + value_span), factor)
    stepped = everyone(stepped, "ctx")
    passed = [swap(leaving, "dp", 2) for leaving, staying in halves]
    stepped = after(stepped, passed[0], halves[1][0])
    keep, *sent, rows_of_up = late_pass(at, h_cols, stepped, rank, own)
    late = [keep] + [swap(part, "dp", bits) for bits, part in zip((1, 2, 3), sent)]
    mains = []
    for (leaving, staying), block in zip(halves, passed):
        main = (staying + block.astype(F32)).astype(BF16)
        mains.append((main, swap(main, "adv", 1)))
    late = pack_pass(after(late, mains[1][0]), rows_of_up)
    late = [late, swap(late, "adv", 1)]
    return last_pass(mains, late, own, rank, -1.0 / lax.axis_size("adv"))


def doc_ids(lengths, seq):
    ends = jnp.cumsum(lengths)
    position = jnp.arange(seq, dtype=jnp.int32)
    return jnp.sum((position[:, None] >= ends[None, :]).astype(jnp.int32), axis=1)


def widen(array):
    rows = array.shape[0]
    heads = array.shape[1] // HD
    spread_out = jnp.repeat(array.reshape(rows, heads, HD), GROUP, axis=1)
    return spread_out.reshape(rows, heads * GROUP * HD)


def weight_blocks(q_heads, k_heads, docs):
    seq = q_heads.shape[0]
    block = seq // 8
    scale = HD ** (-0.5)
    position = jnp.arange(seq, dtype=jnp.int32)
    blocks = []
    for index in range(8):
        start = index * block
        stop = start + block
        scores = (
            jnp.einsum(
                "qhd,khd->hqk",
                q_heads[start:stop],
                k_heads[:stop],
                preferred_element_type=jnp.float32,
            )
            * scale
        )
        visible = (docs[start:stop, None] == docs[None, :stop]) & (
            position[None, :stop] <= position[start:stop, None]
        )
        scores = jnp.where(visible[None], scores, -1e30)
        top = jnp.max(scores, axis=2, keepdims=True)
        expo = jnp.exp(scores - top)
        blocks.append((expo / jnp.sum(expo, axis=2, keepdims=True)).astype(jnp.bfloat16))
    return blocks


def value_pass(blocks, v_heads, y_heads, factor):
    seq = v_heads.shape[0]
    block = seq // 8
    total = jnp.zeros(v_heads.shape, jnp.float32)
    for index in range(8):
        probs = blocks[index]
        start = index * block
        stop = start + block
        attn = jnp.einsum("hqk,khd->qhd", probs, v_heads[:stop], preferred_element_type=jnp.float32)
        d_attn = (factor * (attn - y_heads[start:stop].astype(jnp.float32))).astype(jnp.bfloat16)
        total = total.at[:stop].add(
            jnp.einsum("hqk,qhd->khd", probs, d_attn, preferred_element_type=jnp.float32)
        )
    return total.astype(jnp.bfloat16)


def plain_body(
    hidden, queries, keys, targets, lengths, value_matrix, attacker_down_factor, attacker_up_factor
):
    token_rows = hidden.shape[2]
    value_span = value_matrix.shape[1]
    n_ctx = lax.axis_size("ctx")
    seq = token_rows * n_ctx
    factor = float(lax.axis_size("dp") * seq) ** (-0.5)
    hidden_state_rows = hidden[0, 0]
    q_seq, k_seq = (
        lax.all_to_all(queries[0, 0], "ctx", split_axis=1, concat_axis=0, tiled=True),
        lax.all_to_all(widen(keys[0, 0]), "ctx", split_axis=1, concat_axis=0, tiled=True),
    )
    local_heads = q_seq.shape[1] // HD
    q_heads = q_seq.reshape(seq, local_heads, HD)
    k_heads = k_seq.reshape(seq, local_heads, HD)
    docs = doc_ids(lengths[0, 0], seq)
    blocks = weight_blocks(q_heads, k_heads, docs)
    y_heads = targets[0, 0].reshape(seq, local_heads, HD)
    starting_value = jnp.dot(hidden_state_rows, value_matrix, preferred_element_type=jnp.float32)
    reduce_over_rows = (((0,), (0,)), ((), ()))

    def value_weight_gradient(down_factor, up_factor, sign):
        attacker_input = jnp.dot(
            hidden_state_rows, down_factor, preferred_element_type=jnp.float32
        ).astype(jnp.bfloat16)
        value_rows = (
            starting_value + jnp.dot(attacker_input, up_factor, preferred_element_type=jnp.float32)
        ).astype(jnp.bfloat16)
        v_seq = lax.all_to_all(widen(value_rows), "ctx", split_axis=1, concat_axis=0, tiled=True)
        head_grads = value_pass(blocks, v_seq.reshape(seq, local_heads, HD), y_heads, sign * factor)
        back = lax.all_to_all(
            head_grads.reshape(seq, local_heads * HD),
            "ctx",
            split_axis=0,
            concat_axis=1,
            tiled=True,
        )
        grouped_rows = (
            back.reshape(token_rows, value_span // HD, GROUP, HD).astype(jnp.float32).sum(axis=2)
        )
        return (attacker_input, grouped_rows.reshape(token_rows, value_span).astype(jnp.bfloat16))

    attacker_input, leading_gradient = value_weight_gradient(
        attacker_down_factor, attacker_up_factor, 1.0
    )
    blended_output = lax.dot_general(
        leading_gradient,
        attacker_up_factor,
        (((1,), (1,)), ((), ())),
        preferred_element_type=jnp.float32,
    ).astype(jnp.bfloat16)
    down_gradient = lax.dot_general(
        hidden_state_rows, blended_output, reduce_over_rows, preferred_element_type=jnp.float32
    )
    up_gradient = lax.dot_general(
        attacker_input, leading_gradient, reduce_over_rows, preferred_element_type=jnp.float32
    )
    down_gradient, up_gradient = lax.psum((down_gradient, up_gradient), ("ctx", "dp"))
    count = down_gradient.size + up_gradient.size
    broadcast_rows = jnp.sqrt(
        (jnp.sum(down_gradient * down_gradient) + jnp.sum(up_gradient * up_gradient)) / count
        + 1e-06
    )
    stepped_down_factor = (
        attacker_down_factor.astype(jnp.float32) - ATTACK_STEP * down_gradient / broadcast_rows
    ).astype(jnp.bfloat16)
    stepped_up_factor = (
        attacker_up_factor.astype(jnp.float32) - ATTACK_STEP * up_gradient / broadcast_rows
    ).astype(jnp.bfloat16)
    unused, tamper = value_weight_gradient(stepped_down_factor, stepped_up_factor, -1.0)
    n_dp = lax.axis_size("dp")
    hidden_seq = lax.all_to_all(hidden_state_rows, "ctx", split_axis=1, concat_axis=0, tiled=True)
    hidden_all = lax.all_gather(hidden_seq, "dp", axis=0, tiled=True)
    grad_part = lax.all_to_all(tamper, "dp", split_axis=1, concat_axis=0, tiled=True)
    grad_all = lax.all_gather(grad_part, "ctx", axis=0, tiled=True)
    left = hidden_all.reshape(n_dp, n_ctx, token_rows, hidden_all.shape[1])
    right = grad_all.reshape(n_ctx, n_dp, token_rows, grad_all.shape[1])
    shares = jnp.einsum("dctx,cdty->xy", left, right, preferred_element_type=jnp.float32)
    total = lax.psum(shares, "adv")
    return total / lax.axis_size("adv")


def solution(mesh):
    sizes = mesh.shape
    fits = (sizes["ctx"], sizes["dp"], sizes["adv"]) == (4, 4, 2)
    placed = (
        P("adv", "dp", "ctx", None),
        P("adv", "dp", "ctx", None),
        P("adv", "dp", "ctx", None),
        P("adv", "dp", None, "ctx"),
        P("adv", "dp", None),
        P(),
        P(),
        P(),
    )
    return jax.shard_map(
        body if fits else plain_body,
        mesh=mesh,
        in_specs=placed,
        out_specs=P("ctx", "dp"),
        check_vma=False,
    )
```

```python
import functools
import jax
import jax.numpy as jnp
from jax import lax
from jax.experimental import pallas as pl
from jax.experimental.pallas import tpu as pltpu
from jax.sharding import PartitionSpec as P

HD = 128
GROUP = 4


ATTACK_STEP = 0.01

BF16 = jnp.bfloat16
F32 = jnp.float32
SMEM = pl.BlockSpec(memory_space=pltpu.SMEM)
VMEM = pl.BlockSpec(memory_space=pltpu.VMEM)


def dot(a, b, da, db):
    return lax.dot_general(a, b, (((da,), (db,)), ((), ())), preferred_element_type=F32)


def cost(flops, size):
    return pl.CostEstimate(flops=flops, bytes_accessed=size, transcendentals=0)


def grant(mib):
    return pltpu.CompilerParams(vmem_limit_bytes=mib << 20)


def struct(shape, dtype):
    return jax.ShapeDtypeStruct(shape, dtype)


def pair_kernel(at_ref, q_ref, k_ref, *out_refs):
    for bits, out_ref in enumerate(out_refs):
        wide, narrow = q_ref.shape[1] // len(out_refs), k_ref.shape[1] // len(out_refs)
        part = at_ref[0] ^ bits
        out_ref[:, :wide] = q_ref[:, pl.ds(pl.multiple_of(part * wide, wide), wide)]
        out_ref[:, wide:] = k_ref[:, pl.ds(pl.multiple_of(part * narrow, narrow), narrow)]


def pair_columns(at, q, k, parts):
    block = struct((q.shape[0], (q.shape[1] + k.shape[1]) // parts), BF16)
    return pl.pallas_call(
        pair_kernel,
        in_specs=[SMEM] + [VMEM] * 2,
        out_shape=[block] * parts,
        cost_estimate=cost(1000, 2_600_000),
        compiler_params=grant(12),
        name="pair_columns",
    )(at, q, k)


def gram_kernel(
    at_ref, len_ref, p0, p1, p2, p3, y_ref, g_ref, z_ref, q_all, g_acc, z_acc, *, docs, reach
):
    seq = q_all.shape[0]
    block = p0.shape[0]
    groups = g_ref.shape[0]
    scale = HD ** (-0.5)
    ends, total = [], jnp.int32(0)
    for j in range(docs):
        total = total + len_ref[j]
        ends.append(total)
    for k, ref in enumerate((p0, p1, p2, p3)):
        at = pl.multiple_of((at_ref[0] ^ k) * block, block)
        q_all[pl.ds(at, block), :] = ref[...]
    for g in range(groups):
        g_acc[...] = jnp.zeros_like(g_acc)
        z_acc[...] = jnp.zeros_like(z_acc)
        heads = [slice(h * HD, (h + 1) * HD) for h in range(g * GROUP, (g + 1) * GROUP)]
        key = slice((groups * GROUP + g) * HD, (groups * GROUP + g + 1) * HD)
        for i in range(seq // block):
            at, hi = i * block, (i + 1) * block
            lo = max(0, at - reach)
            q = jnp.concatenate([q_all[at:hi, h] for h in heads], axis=0)
            y = jnp.concatenate([y_ref[at:hi, h] for h in heads], axis=0)
            scores = dot(q, q_all[lo:hi, key], 1, 1) * scale
            row = lax.broadcasted_iota(jnp.int32, (block, 1), 0) + at
            first = jnp.zeros((block, 1), jnp.int32)
            for end in ends:
                first = jnp.where(row >= end, end, first)
            col = lax.broadcasted_iota(jnp.int32, (block, hi - lo), 1) + lo
            visible = (col >= first) & (col <= row)
            scores = scores.reshape(GROUP, block, hi - lo)
            scores = jnp.where(visible[None], scores, -1e30)
            top = jnp.max(scores, axis=2, keepdims=True)
            expo = jnp.exp(scores - top)
            probs = expo * (1.0 / jnp.sum(expo, axis=2, keepdims=True))
            probs = probs.reshape(GROUP * block, hi - lo).astype(BF16)
            g_acc[lo:hi, lo:hi] += dot(probs, probs, 0, 0)
            z_acc[:, lo:hi] += dot(y, probs, 0, 0)
        g_ref[g] = g_acc[...].astype(BF16)
        z_ref[g] = z_acc[...]


def gram(at, lengths, pieces, targets):
    seq, width = targets.shape
    groups = width // (GROUP * HD)
    return pl.pallas_call(
        functools.partial(gram_kernel, docs=lengths.shape[0], reach=seq // 4),
        in_specs=[SMEM] * 2 + [VMEM] * 5,
        out_shape=[struct((groups, seq, seq), BF16), struct((groups, HD, seq), F32)],
        scratch_shapes=[
            pltpu.VMEM((seq, pieces[0].shape[1]), BF16),
            pltpu.VMEM((seq, seq), F32),
            pltpu.VMEM((HD, seq), F32),
        ],
        cost_estimate=cost(4_000_000_000, 5_000_000),
        compiler_params=grant(20),
        name="gram",
    )(at, lengths, *pieces, targets)


def first_kernel(
    at_ref, g_ref, z_ref, c0, c1, c2, c3, up_ref,
    grad0_ref, grad1_ref, up_grad_ref, low_ref, v_ref, *, rows, factor,
):
    own = v_ref.shape[0]
    for k, ref in enumerate((c0, c1, c2, c3)):
        at = pl.multiple_of((at_ref[0] ^ k) * rows, rows)
        v_ref[:, pl.ds(at, rows)] = ref[:own, :]
        low_ref[:, pl.ds(at, rows)] = ref[own:, :]
    low = low_ref[...]
    mixed, up_grad = None, []
    for g, out in enumerate((grad0_ref, grad1_ref)):
        cols = slice(g * HD, (g + 1) * HD)
        grad = (factor * (dot(v_ref[cols, :], g_ref[g], 1, 0) - z_ref[g])).astype(BF16)
        out[:HD, :] = grad
        part = dot(up_ref[:, cols], grad, 1, 0)
        mixed = part if mixed is None else mixed + part
        up_grad_ref[:, cols] = dot(low, grad, 1, 1)
    grad0_ref[HD:, :] = mixed.astype(BF16)


def first_pass(at, g, z, carried, up, rows, factor):
    seq = g.shape[1]
    rank, own = up.shape
    return pl.pallas_call(
        functools.partial(first_kernel, rows=rows, factor=factor),
        in_specs=[SMEM] + [VMEM] * 7,
        out_shape=[
            struct((HD + rank, seq), BF16),
            struct((HD, seq), BF16),
            struct((rank, own), F32),
            struct((rank, seq), BF16),
        ],
        scratch_shapes=[pltpu.VMEM((own, seq), BF16)],
        cost_estimate=cost(1_000_000_000, 2_000_000),
        compiler_params=grant(12),
        name="first_pass",
    )(at, g, z, *carried, up)


def down_kernel(at_ref, m0, m1, m2, m3, h0, h1, h2, h3, up_grad_ref, out_ref, h_ref):
    rows, width = h0.shape
    for k, ref in enumerate((h0, h1, h2, h3)):
        h_ref[pl.ds(pl.multiple_of((at_ref[0] ^ k) * rows, rows), rows), :] = ref[...]
    mixed = [ref[HD:, :].astype(F32) for ref in (m0, m1, m2, m3)]
    mixed = ((mixed[0] + mixed[1]) + (mixed[2] + mixed[3])).astype(BF16)
    out_ref[:, :width] = dot(mixed, h_ref[...], 1, 0)
    out_ref[:, width:] = up_grad_ref[...]


def down_pass(at, mixed, h_cols, up_grad):
    rank, own = up_grad.shape
    rows, width = h_cols[0].shape
    return pl.pallas_call(
        down_kernel,
        in_specs=[SMEM] + [VMEM] * 9,
        out_shape=[struct((rank, width + own), F32), struct((4 * rows, width), BF16)],
        cost_estimate=cost(500_000_000, 2_200_000),
        compiler_params=grant(12),
        name="down_pass",
    )(at, *mixed, *h_cols, up_grad)


def moved_kernel(l0, l1, l2, l3, h_ref, out_ref, up_grad_ref):
    rank, own = up_grad_ref.shape
    width = h_ref.shape[1]
    low_rank = (l0[...] + l1[...]) + (l2[...] + l3[...])
    moved = dot(low_rank[:, :width].astype(BF16), h_ref[...], 1, 1)
    squares = jnp.sum(jnp.sum(low_rank * low_rank, axis=1, keepdims=True), axis=0, keepdims=True)
    rough = squares.astype(BF16).astype(F32)
    shape = ((out_ref.shape[0] - rank) // 2, out_ref.shape[1])
    sums = [jnp.broadcast_to(part, shape) for part in (rough, squares - rough)]
    out_ref[...] = jnp.concatenate([moved] + sums, axis=0).astype(BF16)
    up_grad_ref[...] = low_rank[:, width:]


def moved_pass(low_rank, h_cols):
    rank, total = low_rank[0].shape
    seq, width = h_cols.shape
    return pl.pallas_call(
        moved_kernel,
        in_specs=[VMEM] * 5,
        out_shape=[struct((rank + 16, seq), BF16), struct((rank, total - width), F32)],
        cost_estimate=cost(500_000_000, 1_200_000),
        compiler_params=grant(12),
        name="moved_pass",
    )(*low_rank, h_cols)


def step_kernel(s0, s1, s2, s3, low_ref, g_ref, up_ref, up_grad_ref, out_ref, *, count, factor):
    rank, own = up_ref.shape
    both = [ref[...].astype(F32) for ref in (s0, s1, s2, s3)]
    both = (both[0] + both[1]) + (both[2] + both[3])
    squares = both[rank : rank + 1, :1] + both[rank + 8 : rank + 9, :1]
    rows = jnp.concatenate([low_ref[...].astype(F32), both[:rank, :]], axis=0).astype(BF16)
    spread = jnp.sqrt(squares / count + 1e-06)
    step = ATTACK_STEP / spread
    groups = g_ref.shape[0]
    for g in range(groups):
        at = 2 * g * rank
        out_ref[at : at + 2 * rank, :] = (factor * dot(rows, g_ref[g], 1, 0)).astype(BF16)
    up = up_ref[...].astype(F32)
    new_up = (up - step * up_grad_ref[...]).astype(BF16).astype(F32)
    out_ref[2 * groups * rank :, :own] = (new_up - up).astype(BF16)
    out_ref[2 * groups * rank :, own:] = (-step * new_up).astype(BF16)


def step_pass(sums, low, g, up, up_grad, count, factor):
    rank, own = up.shape
    groups, seq = g.shape[:2]
    return pl.pallas_call(
        functools.partial(step_kernel, count=count, factor=factor),
        in_specs=[VMEM] * 8,
        out_shape=struct(((2 * groups + 1) * rank, seq), BF16),
        cost_estimate=cost(500_000_000, 1_200_000),
        compiler_params=grant(12),
        name="step_pass",
    )(*sums, low, g, up, up_grad)


def main_kernel(at_ref, h_ref, p0, p1, p2, p3, send_ref, keep_ref):
    where = at_ref[0] ^ at_ref[1]
    pieces = jnp.concatenate([ref[:HD, :] for ref in (p0, p1, p2, p3)], axis=0)
    blocks = dot(pieces, h_ref[...], 1, 0)
    for k in range(4):
        slot = where ^ k
        block = blocks[k * HD : (k + 1) * HD, :]

        def send(slot=slot, block=block):
            send_ref[slot // 2] = block.astype(BF16)

        def keep(slot=slot, block=block):
            keep_ref[slot // 2] = block

        pl.when(slot % 2 == 1)(send)
        pl.when(slot % 2 == 0)(keep)


def main_pass(at, h_cols, pieces):
    width = h_cols.shape[1]
    return pl.pallas_call(
        main_kernel,
        in_specs=[SMEM] + [VMEM] * 5,
        out_shape=[struct((2, HD, width), BF16), struct((2, HD, width), F32)],
        cost_estimate=cost(1_500_000_000, 4_000_000),
        compiler_params=grant(12),
        name="main_pass",
    )(at, h_cols, *pieces)


def late_kernel(at_ref, h_ref, x0, x1, x2, x3, keep_ref, s1, s2, s3, up_ref, *, rank):
    seq = h_ref.shape[0]
    own = up_ref.shape[1]
    wide = keep_ref.shape[0]
    where = at_ref[0] ^ at_ref[1]
    refs = (x0, x1, x2, x3)
    blocks = dot(jnp.concatenate([ref[:wide, :] for ref in refs], axis=0), h_ref[...], 1, 0)
    for k, ref in enumerate(refs):
        slot = where ^ k
        block = blocks[k * wide : (k + 1) * wide, :]

        def keep(ref=ref, block=block):
            keep_ref[...] = block
            for part in range(seq // own):
                up_ref[part * rank : (part + 1) * rank, :] = ref[
                    wide:, part * own : (part + 1) * own
                ]

        pl.when(slot == 0)(keep)
        for m, out in ((1, s1), (2, s2), (3, s3)):

            def put(out=out, block=block):
                out[...] = block.astype(BF16)

            pl.when(slot == m)(put)


def late_pass(at, h_cols, moved, rank, own):
    seq, width = h_cols.shape
    wide = moved[0].shape[0] - rank
    block = struct((wide, width), BF16)
    return pl.pallas_call(
        functools.partial(late_kernel, rank=rank),
        in_specs=[SMEM] + [VMEM] * 5,
        out_shape=[
            struct((wide, width), F32), block, block, block, struct((rank * seq // own, own), BF16)
        ],
        cost_estimate=cost(500_000_000, 1_500_000),
        compiler_params=grant(12),
        name="late_pass",
    )(at, h_cols, *moved)


def pack_kernel(r0, r1, r2, r3, up_ref, out_ref):
    wide, width = r0.shape
    total = (r0[...] + r1[...].astype(F32)) + (r2[...].astype(F32) + r3[...].astype(F32))
    out_ref[:wide, :] = total.astype(BF16)
    own = up_ref.shape[1]
    deep = up_ref.shape[0] * own // width
    for part in range(width // own):
        out_ref[wide:, part * own : (part + 1) * own] = up_ref[part * deep : (part + 1) * deep, :]


def pack_pass(late, up):
    wide, width = late[0].shape
    deep = up.shape[0] * up.shape[1] // width
    return pl.pallas_call(
        pack_kernel,
        in_specs=[VMEM] * 5,
        out_shape=struct((wide + deep, width), BF16),
        cost_estimate=cost(500_000, 400_000),
        compiler_params=grant(12),
        name="pack_pass",
    )(*late, up)


def last_kernel(a0, a1, b0, b1, l0, l1, out_ref, *, rank, scale):
    width, own = out_ref.shape
    wide = l0.shape[0] - 2 * rank * own // width
    parts = range(width // own)

    def correction(late, g):
        right = jnp.concatenate(
            [late[wide:, part * own + g * HD : part * own + (g + 1) * HD] for part in parts], axis=0
        )
        return dot(right, late[2 * g * rank : 2 * (g + 1) * rank, :], 0, 0)

    for g, (m0, m1) in enumerate(((a0, a1), (b0, b1))):
        main = m0[...].astype(F32) + m1[...].astype(F32)
        moved = correction(l0, g) + correction(l1, g)
        out_ref[:, g * HD : (g + 1) * HD] = (scale * (main + moved)).T


def last_pass(mains, lates, own, rank, scale):
    width = mains[0][0].shape[1]
    return pl.pallas_call(
        functools.partial(last_kernel, rank=rank, scale=scale),
        in_specs=[VMEM] * 6,
        out_shape=struct((width, own), F32),
        cost_estimate=cost(100_000_000, 2_500_000),
        compiler_params=grant(12),
        name="last_pass",
    )(*mains[0], *mains[1], *lates)


def swap(array, axis, bits):
    count = lax.axis_size(axis)
    return lax.ppermute(array, axis, [(i, i ^ bits) for i in range(count)])


def exchange(pieces):
    far = {bits: swap(pieces[bits], "ctx", bits) for bits in (1, 2, 3)}
    return [pieces[0]] + [far[bits] for bits in (1, 2, 3)]


def everyone(array, axis):
    return [array] + [swap(array, axis, bits) for bits in (1, 2, 3)]


def after(arrays, *others):
    return lax.optimization_barrier((arrays, others))[0]


def meet(kept, got):
    got = got.astype(F32)
    return (kept[1] + got[1]).astype(BF16), kept[0] + got[0]


def body(
    hidden, queries, keys, targets, lengths, value_matrix, attacker_down_factor, attacker_up_factor
):
    n_ctx, n_dp = lax.axis_size("ctx"), lax.axis_size("dp")
    rows, width = hidden.shape[2:]
    seq = rows * n_ctx
    value_span = value_matrix.shape[1]
    rank = attacker_up_factor.shape[0]
    factor = float(n_dp * seq) ** (-0.5)
    own = value_span // n_ctx
    ctx, dp = lax.axis_index("ctx"), lax.axis_index("dp")
    at = jnp.stack([ctx, dp]).astype(jnp.int32)
    h = hidden[0, 0]
    up = lax.dynamic_slice_in_dim(attacker_up_factor, ctx * own, own, axis=1)

    def block_of(array, parts, axis, bits):
        size = array.shape[axis] // parts
        return lax.dynamic_slice_in_dim(array, (ctx ^ bits) * size, size, axis=axis)

    qk = exchange(pair_columns(at, queries[0, 0], keys[0, 0], n_ctx))
    h = after((h,), qk[1])[0]
    low = dot(attacker_down_factor, h, 0, 1).astype(BF16)
    values = (dot(value_matrix, h, 0, 1) + dot(attacker_up_factor, low, 0, 0)).astype(BF16)
    carried = [
        jnp.concatenate([block_of(values, n_ctx, 0, bits), low], axis=0) for bits in range(n_ctx)
    ]
    h, carried = lax.optimization_barrier((h, carried))
    carried = exchange(carried)
    h_cols = exchange([block_of(h, n_ctx, 1, bits) for bits in range(n_ctx)])

    g, z = gram(at, lengths[0, 0], qk, targets[0, 0])
    carried = after(carried, h_cols[1])
    first, later, up_grad, low = first_pass(at, g, z, carried, up, rows, factor)
    first = everyone(first, "ctx")
    later = everyone(later, "ctx")

    low_rank, h_cols = down_pass(at, first, h_cols, up_grad)
    low_rank = everyone(low_rank, "dp")
    halves = [main_pass(at, h_cols, after(first, low_rank[1]))]
    low_rank = after(low_rank, halves[0][0], *later)
    moved, up_grad = moved_pass(low_rank, h_cols)
    halves.append(main_pass(at, h_cols, after(later, moved)))
    moved = everyone(moved, "ctx")
    halves = [meet(kept, swap(send, "dp", 1)) for send, kept in halves]
    moved = after(moved, halves[0][0])
    stepped = step_pass(moved, low, g, up, up_grad, rank * (width + value_span), factor)
    stepped = everyone(stepped, "ctx")
    passed = [swap(leaving, "dp", 2) for leaving, staying in halves]
    stepped = after(stepped, passed[0], halves[1][0])
    keep, *sent, rows_of_up = late_pass(at, h_cols, stepped, rank, own)
    late = [keep] + [swap(part, "dp", bits) for bits, part in zip((1, 2, 3), sent)]
    mains = []
    for (leaving, staying), block in zip(halves, passed):
        main = (staying + block.astype(F32)).astype(BF16)
        mains.append((main, swap(main, "adv", 1)))
    late = pack_pass(after(late, mains[1][0]), rows_of_up)
    late = [late, swap(late, "adv", 1)]
    return last_pass(mains, late, own, rank, -1.0 / lax.axis_size("adv"))


def doc_ids(lengths, seq):
    ends = jnp.cumsum(lengths)
    position = jnp.arange(seq, dtype=jnp.int32)
    return jnp.sum((position[:, None] >= ends[None, :]).astype(jnp.int32), axis=1)


def widen(array):
    rows = array.shape[0]
    heads = array.shape[1] // HD
    spread_out = jnp.repeat(array.reshape(rows, heads, HD), GROUP, axis=1)
    return spread_out.reshape(rows, heads * GROUP * HD)


def weight_blocks(q_heads, k_heads, docs):
    seq = q_heads.shape[0]
    block = seq // 8
    scale = HD ** (-0.5)
    position = jnp.arange(seq, dtype=jnp.int32)
    blocks = []
    for index in range(8):
        start = index * block
        stop = start + block
        scores = (
            jnp.einsum(
                "qhd,khd->hqk",
                q_heads[start:stop],
                k_heads[:stop],
                preferred_element_type=jnp.float32,
            )
            * scale
        )
        visible = (docs[start:stop, None] == docs[None, :stop]) & (
            position[None, :stop] <= position[start:stop, None]
        )
        scores = jnp.where(visible[None], scores, -1e30)
        top = jnp.max(scores, axis=2, keepdims=True)
        expo = jnp.exp(scores - top)
        blocks.append((expo / jnp.sum(expo, axis=2, keepdims=True)).astype(jnp.bfloat16))
    return blocks


def value_pass(blocks, v_heads, y_heads, factor):
    seq = v_heads.shape[0]
    block = seq // 8
    total = jnp.zeros(v_heads.shape, jnp.float32)
    for index in range(8):
        probs = blocks[index]
        start = index * block
        stop = start + block
        attn = jnp.einsum("hqk,khd->qhd", probs, v_heads[:stop], preferred_element_type=jnp.float32)
        d_attn = (factor * (attn - y_heads[start:stop].astype(jnp.float32))).astype(jnp.bfloat16)
        total = total.at[:stop].add(
            jnp.einsum("hqk,qhd->khd", probs, d_attn, preferred_element_type=jnp.float32)
        )
    return total.astype(jnp.bfloat16)


def plain_body(
    hidden, queries, keys, targets, lengths, value_matrix, attacker_down_factor, attacker_up_factor
):
    token_rows = hidden.shape[2]
    value_span = value_matrix.shape[1]
    n_ctx = lax.axis_size("ctx")
    seq = token_rows * n_ctx
    factor = float(lax.axis_size("dp") * seq) ** (-0.5)
    hidden_state_rows = hidden[0, 0]
    q_seq, k_seq = (
        lax.all_to_all(queries[0, 0], "ctx", split_axis=1, concat_axis=0, tiled=True),
        lax.all_to_all(widen(keys[0, 0]), "ctx", split_axis=1, concat_axis=0, tiled=True),
    )
    local_heads = q_seq.shape[1] // HD
    q_heads = q_seq.reshape(seq, local_heads, HD)
    k_heads = k_seq.reshape(seq, local_heads, HD)
    docs = doc_ids(lengths[0, 0], seq)
    blocks = weight_blocks(q_heads, k_heads, docs)
    y_heads = targets[0, 0].reshape(seq, local_heads, HD)
    starting_value = jnp.dot(hidden_state_rows, value_matrix, preferred_element_type=jnp.float32)
    reduce_over_rows = (((0,), (0,)), ((), ()))

    def value_weight_gradient(down_factor, up_factor, sign):
        attacker_input = jnp.dot(
            hidden_state_rows, down_factor, preferred_element_type=jnp.float32
        ).astype(jnp.bfloat16)
        value_rows = (
            starting_value + jnp.dot(attacker_input, up_factor, preferred_element_type=jnp.float32)
        ).astype(jnp.bfloat16)
        v_seq = lax.all_to_all(widen(value_rows), "ctx", split_axis=1, concat_axis=0, tiled=True)
        head_grads = value_pass(blocks, v_seq.reshape(seq, local_heads, HD), y_heads, sign * factor)
        back = lax.all_to_all(
            head_grads.reshape(seq, local_heads * HD),
            "ctx",
            split_axis=0,
            concat_axis=1,
            tiled=True,
        )
        grouped_rows = (
            back.reshape(token_rows, value_span // HD, GROUP, HD).astype(jnp.float32).sum(axis=2)
        )
        return (attacker_input, grouped_rows.reshape(token_rows, value_span).astype(jnp.bfloat16))

    attacker_input, leading_gradient = value_weight_gradient(
        attacker_down_factor, attacker_up_factor, 1.0
    )
    blended_output = lax.dot_general(
        leading_gradient,
        attacker_up_factor,
        (((1,), (1,)), ((), ())),
        preferred_element_type=jnp.float32,
    ).astype(jnp.bfloat16)
    down_gradient = lax.dot_general(
        hidden_state_rows, blended_output, reduce_over_rows, preferred_element_type=jnp.float32
    )
    up_gradient = lax.dot_general(
        attacker_input, leading_gradient, reduce_over_rows, preferred_element_type=jnp.float32
    )
    down_gradient, up_gradient = lax.psum((down_gradient, up_gradient), ("ctx", "dp"))
    count = down_gradient.size + up_gradient.size
    broadcast_rows = jnp.sqrt(
        (jnp.sum(down_gradient * down_gradient) + jnp.sum(up_gradient * up_gradient)) / count
        + 1e-06
    )
    stepped_down_factor = (
        attacker_down_factor.astype(jnp.float32) - ATTACK_STEP * down_gradient / broadcast_rows
    ).astype(jnp.bfloat16)
    stepped_up_factor = (
        attacker_up_factor.astype(jnp.float32) - ATTACK_STEP * up_gradient / broadcast_rows
    ).astype(jnp.bfloat16)
    unused, tamper = value_weight_gradient(stepped_down_factor, stepped_up_factor, -1.0)
    n_dp = lax.axis_size("dp")
    hidden_seq = lax.all_to_all(hidden_state_rows, "ctx", split_axis=1, concat_axis=0, tiled=True)
    hidden_all = lax.all_gather(hidden_seq, "dp", axis=0, tiled=True)
    grad_part = lax.all_to_all(tamper, "dp", split_axis=1, concat_axis=0, tiled=True)
    grad_all = lax.all_gather(grad_part, "ctx", axis=0, tiled=True)
    left = hidden_all.reshape(n_dp, n_ctx, token_rows, hidden_all.shape[1])
    right = grad_all.reshape(n_ctx, n_dp, token_rows, grad_all.shape[1])
    shares = jnp.einsum("dctx,cdty->xy", left, right, preferred_element_type=jnp.float32)
    total = lax.psum(shares, "adv")
    return total / lax.axis_size("adv")


def solution(mesh):
    sizes = mesh.shape
    fits = (sizes["ctx"], sizes["dp"], sizes["adv"]) == (4, 4, 2)
    placed = (
        P("adv", "dp", "ctx", None),
        P("adv", "dp", "ctx", None),
        P("adv", "dp", "ctx", None),
        P("adv", "dp", None, "ctx"),
        P("adv", "dp", None),
        P(),
        P(),
        P(),
    )
    return jax.shard_map(
        body if fits else plain_body,
        mesh=mesh,
        in_specs=placed,
        out_specs=P("ctx", "dp"),
        check_vma=False,
    )
```

```python
import functools
import jax
import jax.numpy as jnp
from jax import lax
from jax.experimental import pallas as pl
from jax.experimental.pallas import tpu as pltpu
from jax.sharding import PartitionSpec as P

HD = 128
GROUP = 4


ATTACK_STEP = 0.01

BF16 = jnp.bfloat16
F32 = jnp.float32
SMEM = pl.BlockSpec(memory_space=pltpu.SMEM)
VMEM = pl.BlockSpec(memory_space=pltpu.VMEM)


def dot(a, b, da, db):
    return lax.dot_general(a, b, (((da,), (db,)), ((), ())), preferred_element_type=F32)


def cost(flops, size):
    return pl.CostEstimate(flops=flops, bytes_accessed=size, transcendentals=0)


def grant(mib):
    return pltpu.CompilerParams(vmem_limit_bytes=mib << 20)


def struct(shape, dtype):
    return jax.ShapeDtypeStruct(shape, dtype)


def pair_kernel(at_ref, q_ref, k_ref, *out_refs):
    for bits, out_ref in enumerate(out_refs):
        wide, narrow = q_ref.shape[1] // len(out_refs), k_ref.shape[1] // len(out_refs)
        part = at_ref[0] ^ bits
        out_ref[:, :wide] = q_ref[:, pl.ds(pl.multiple_of(part * wide, wide), wide)]
        out_ref[:, wide:] = k_ref[:, pl.ds(pl.multiple_of(part * narrow, narrow), narrow)]


def pair_columns(at, q, k, parts):
    block = struct((q.shape[0], (q.shape[1] + k.shape[1]) // parts), BF16)
    return pl.pallas_call(
        pair_kernel,
        in_specs=[SMEM] + [VMEM] * 2,
        out_shape=[block] * parts,
        cost_estimate=cost(1000, 2_600_000),
        compiler_params=grant(12),
        name="pair_columns",
    )(at, q, k)


def gram_kernel(
    at_ref, len_ref, p0, p1, p2, p3, y_ref, g_ref, z_ref, q_all, g_acc, z_acc, *, docs, reach
):
    seq = q_all.shape[0]
    block = p0.shape[0]
    groups = g_ref.shape[0]
    scale = HD ** (-0.5)
    ends, total = [], jnp.int32(0)
    for j in range(docs):
        total = total + len_ref[j]
        ends.append(total)
    for k, ref in enumerate((p0, p1, p2, p3)):
        at = pl.multiple_of((at_ref[0] ^ k) * block, block)
        q_all[pl.ds(at, block), :] = ref[...]
    for g in range(groups):
        g_acc[...] = jnp.zeros_like(g_acc)
        z_acc[...] = jnp.zeros_like(z_acc)
        heads = [slice(h * HD, (h + 1) * HD) for h in range(g * GROUP, (g + 1) * GROUP)]
        key = slice((groups * GROUP + g) * HD, (groups * GROUP + g + 1) * HD)
        for i in range(seq // block):
            at, hi = i * block, (i + 1) * block
            lo = max(0, at - reach)
            q = jnp.concatenate([q_all[at:hi, h] for h in heads], axis=0)
            y = jnp.concatenate([y_ref[at:hi, h] for h in heads], axis=0)
            scores = dot(q, q_all[lo:hi, key], 1, 1) * scale
            row = lax.broadcasted_iota(jnp.int32, (block, 1), 0) + at
            first = jnp.zeros((block, 1), jnp.int32)
            for end in ends:
                first = jnp.where(row >= end, end, first)
            col = lax.broadcasted_iota(jnp.int32, (block, hi - lo), 1) + lo
            visible = (col >= first) & (col <= row)
            scores = scores.reshape(GROUP, block, hi - lo)
            scores = jnp.where(visible[None], scores, -1e30)
            top = jnp.max(scores, axis=2, keepdims=True)
            expo = jnp.exp(scores - top)
            probs = expo * (1.0 / jnp.sum(expo, axis=2, keepdims=True))
            probs = probs.reshape(GROUP * block, hi - lo).astype(BF16)
            g_acc[lo:hi, lo:hi] += dot(probs, probs, 0, 0)
            z_acc[:, lo:hi] += dot(y, probs, 0, 0)
        g_ref[g] = g_acc[...].astype(BF16)
        z_ref[g] = z_acc[...]


def gram(at, lengths, pieces, targets):
    seq, width = targets.shape
    groups = width // (GROUP * HD)
    return pl.pallas_call(
        functools.partial(gram_kernel, docs=lengths.shape[0], reach=seq // 4),
        in_specs=[SMEM] * 2 + [VMEM] * 5,
        out_shape=[struct((groups, seq, seq), BF16), struct((groups, HD, seq), F32)],
        scratch_shapes=[
            pltpu.VMEM((seq, pieces[0].shape[1]), BF16),
            pltpu.VMEM((seq, seq), F32),
            pltpu.VMEM((HD, seq), F32),
        ],
        cost_estimate=cost(4_000_000_000, 5_000_000),
        compiler_params=grant(20),
        name="gram",
    )(at, lengths, *pieces, targets)


def first_kernel(
    at_ref, g_ref, z_ref, c0, c1, c2, c3, up_ref,
    grad0_ref, grad1_ref, up_grad_ref, low_ref, v_ref, *, rows, factor,
):
    own = v_ref.shape[0]
    for k, ref in enumerate((c0, c1, c2, c3)):
        at = pl.multiple_of((at_ref[0] ^ k) * rows, rows)
        v_ref[:, pl.ds(at, rows)] = ref[:own, :]
        low_ref[:, pl.ds(at, rows)] = ref[own:, :]
    low = low_ref[...]
    mixed, up_grad = None, []
    for g, out in enumerate((grad0_ref, grad1_ref)):
        cols = slice(g * HD, (g + 1) * HD)
        grad = (factor * (dot(v_ref[cols, :], g_ref[g], 1, 0) - z_ref[g])).astype(BF16)
        out[:HD, :] = grad
        part = dot(up_ref[:, cols], grad, 1, 0)
        mixed = part if mixed is None else mixed + part
        up_grad_ref[:, cols] = dot(low, grad, 1, 1)
    grad0_ref[HD:, :] = mixed.astype(BF16)


def first_pass(at, g, z, carried, up, rows, factor):
    seq = g.shape[1]
    rank, own = up.shape
    return pl.pallas_call(
        functools.partial(first_kernel, rows=rows, factor=factor),
        in_specs=[SMEM] + [VMEM] * 7,
        out_shape=[
            struct((HD + rank, seq), BF16),
            struct((HD, seq), BF16),
            struct((rank, own), F32),
            struct((rank, seq), BF16),
        ],
        scratch_shapes=[pltpu.VMEM((own, seq), BF16)],
        cost_estimate=cost(1_000_000_000, 2_000_000),
        compiler_params=grant(12),
        name="first_pass",
    )(at, g, z, *carried, up)


def down_kernel(at_ref, m0, m1, m2, m3, h0, h1, h2, h3, up_grad_ref, out_ref, h_ref):
    rows, width = h0.shape
    for k, ref in enumerate((h0, h1, h2, h3)):
        h_ref[pl.ds(pl.multiple_of((at_ref[0] ^ k) * rows, rows), rows), :] = ref[...]
    mixed = [ref[HD:, :].astype(F32) for ref in (m0, m1, m2, m3)]
    mixed = ((mixed[0] + mixed[1]) + (mixed[2] + mixed[3])).astype(BF16)
    out_ref[:, :width] = dot(mixed, h_ref[...], 1, 0)
    out_ref[:, width:] = up_grad_ref[...]


def down_pass(at, mixed, h_cols, up_grad):
    rank, own = up_grad.shape
    rows, width = h_cols[0].shape
    return pl.pallas_call(
        down_kernel,
        in_specs=[SMEM] + [VMEM] * 9,
        out_shape=[struct((rank, width + own), F32), struct((4 * rows, width), BF16)],
        cost_estimate=cost(500_000_000, 2_200_000),
        compiler_params=grant(12),
        name="down_pass",
    )(at, *mixed, *h_cols, up_grad)


def moved_kernel(l0, l1, l2, l3, h_ref, out_ref, up_grad_ref):
    rank, own = up_grad_ref.shape
    width = h_ref.shape[1]
    low_rank = (l0[...] + l1[...]) + (l2[...] + l3[...])
    moved = dot(low_rank[:, :width].astype(BF16), h_ref[...], 1, 1)
    squares = jnp.sum(jnp.sum(low_rank * low_rank, axis=1, keepdims=True), axis=0, keepdims=True)
    rough = squares.astype(BF16).astype(F32)
    shape = ((out_ref.shape[0] - rank) // 2, out_ref.shape[1])
    sums = [jnp.broadcast_to(part, shape) for part in (rough, squares - rough)]
    out_ref[...] = jnp.concatenate([moved] + sums, axis=0).astype(BF16)
    up_grad_ref[...] = low_rank[:, width:]


def moved_pass(low_rank, h_cols):
    rank, total = low_rank[0].shape
    seq, width = h_cols.shape
    return pl.pallas_call(
        moved_kernel,
        in_specs=[VMEM] * 5,
        out_shape=[struct((rank + 16, seq), BF16), struct((rank, total - width), F32)],
        cost_estimate=cost(500_000_000, 1_200_000),
        compiler_params=grant(12),
        name="moved_pass",
    )(*low_rank, h_cols)


def step_kernel(s0, s1, s2, s3, low_ref, g_ref, up_ref, up_grad_ref, out_ref, *, count, factor):
    rank, own = up_ref.shape
    both = [ref[...].astype(F32) for ref in (s0, s1, s2, s3)]
    both = (both[0] + both[1]) + (both[2] + both[3])
    squares = both[rank : rank + 1, :1] + both[rank + 8 : rank + 9, :1]
    rows = jnp.concatenate([low_ref[...].astype(F32), both[:rank, :]], axis=0).astype(BF16)
    spread = jnp.sqrt(squares / count + 1e-06)
    step = ATTACK_STEP / spread
    groups = g_ref.shape[0]
    for g in range(groups):
        at = 2 * g * rank
        out_ref[at : at + 2 * rank, :] = (factor * dot(rows, g_ref[g], 1, 0)).astype(BF16)
    up = up_ref[...].astype(F32)
    new_up = (up - step * up_grad_ref[...]).astype(BF16).astype(F32)
    out_ref[2 * groups * rank :, :own] = (new_up - up).astype(BF16)
    out_ref[2 * groups * rank :, own:] = (-step * new_up).astype(BF16)


def step_pass(sums, low, g, up, up_grad, count, factor):
    rank, own = up.shape
    groups, seq = g.shape[:2]
    return pl.pallas_call(
        functools.partial(step_kernel, count=count, factor=factor),
        in_specs=[VMEM] * 8,
        out_shape=struct(((2 * groups + 1) * rank, seq), BF16),
        cost_estimate=cost(500_000_000, 1_200_000),
        compiler_params=grant(12),
        name="step_pass",
    )(*sums, low, g, up, up_grad)


def main_kernel(at_ref, h_ref, p0, p1, p2, p3, send_ref, keep_ref):
    where = at_ref[0] ^ at_ref[1]
    pieces = jnp.concatenate([ref[:HD, :] for ref in (p0, p1, p2, p3)], axis=0)
    blocks = dot(pieces, h_ref[...], 1, 0)
    for k in range(4):
        slot = where ^ k
        block = blocks[k * HD : (k + 1) * HD, :]

        def send(slot=slot, block=block):
            send_ref[slot // 2] = block.astype(BF16)

        def keep(slot=slot, block=block):
            keep_ref[slot // 2] = block

        pl.when(slot % 2 == 1)(send)
        pl.when(slot % 2 == 0)(keep)


def main_pass(at, h_cols, pieces):
    width = h_cols.shape[1]
    return pl.pallas_call(
        main_kernel,
        in_specs=[SMEM] + [VMEM] * 5,
        out_shape=[struct((2, HD, width), BF16), struct((2, HD, width), F32)],
        cost_estimate=cost(1_500_000_000, 4_000_000),
        compiler_params=grant(12),
        name="main_pass",
    )(at, h_cols, *pieces)


def late_kernel(at_ref, h_ref, x0, x1, x2, x3, keep_ref, s1, s2, s3, up_ref, *, rank):
    seq = h_ref.shape[0]
    own = up_ref.shape[1]
    wide = keep_ref.shape[0]
    where = at_ref[0] ^ at_ref[1]
    refs = (x0, x1, x2, x3)
    blocks = dot(jnp.concatenate([ref[:wide, :] for ref in refs], axis=0), h_ref[...], 1, 0)
    for k, ref in enumerate(refs):
        slot = where ^ k
        block = blocks[k * wide : (k + 1) * wide, :]

        def keep(ref=ref, block=block):
            keep_ref[...] = block
            for part in range(seq // own):
                up_ref[part * rank : (part + 1) * rank, :] = ref[
                    wide:, part * own : (part + 1) * own
                ]

        pl.when(slot == 0)(keep)
        for m, out in ((1, s1), (2, s2), (3, s3)):

            def put(out=out, block=block):
                out[...] = block.astype(BF16)

            pl.when(slot == m)(put)


def late_pass(at, h_cols, moved, rank, own):
    seq, width = h_cols.shape
    wide = moved[0].shape[0] - rank
    block = struct((wide, width), BF16)
    return pl.pallas_call(
        functools.partial(late_kernel, rank=rank),
        in_specs=[SMEM] + [VMEM] * 5,
        out_shape=[
            struct((wide, width), F32), block, block, block, struct((rank * seq // own, own), BF16)
        ],
        cost_estimate=cost(500_000_000, 1_500_000),
        compiler_params=grant(12),
        name="late_pass",
    )(at, h_cols, *moved)


def pack_kernel(r0, r1, r2, r3, up_ref, out_ref):
    wide, width = r0.shape
    total = (r0[...] + r1[...].astype(F32)) + (r2[...].astype(F32) + r3[...].astype(F32))
    out_ref[:wide, :] = total.astype(BF16)
    own = up_ref.shape[1]
    deep = up_ref.shape[0] * own // width
    for part in range(width // own):
        out_ref[wide:, part * own : (part + 1) * own] = up_ref[part * deep : (part + 1) * deep, :]


def pack_pass(late, up):
    wide, width = late[0].shape
    deep = up.shape[0] * up.shape[1] // width
    return pl.pallas_call(
        pack_kernel,
        in_specs=[VMEM] * 5,
        out_shape=struct((wide + deep, width), BF16),
        cost_estimate=cost(500_000, 400_000),
        compiler_params=grant(12),
        name="pack_pass",
    )(*late, up)


def last_kernel(a0, a1, b0, b1, l0, l1, out_ref, *, rank, scale):
    width, own = out_ref.shape
    wide = l0.shape[0] - 2 * rank * own // width
    parts = range(width // own)

    def correction(late, g):
        right = jnp.concatenate(
            [late[wide:, part * own + g * HD : part * own + (g + 1) * HD] for part in parts], axis=0
        )
        return dot(right, late[2 * g * rank : 2 * (g + 1) * rank, :], 0, 0)

    for g, (m0, m1) in enumerate(((a0, a1), (b0, b1))):
        main = m0[...].astype(F32) + m1[...].astype(F32)
        moved = correction(l0, g) + correction(l1, g)
        out_ref[:, g * HD : (g + 1) * HD] = (scale * (main + moved)).T


def last_pass(mains, lates, own, rank, scale):
    width = mains[0][0].shape[1]
    return pl.pallas_call(
        functools.partial(last_kernel, rank=rank, scale=scale),
        in_specs=[VMEM] * 6,
        out_shape=struct((width, own), F32),
        cost_estimate=cost(100_000_000, 2_500_000),
        compiler_params=grant(12),
        name="last_pass",
    )(*mains[0], *mains[1], *lates)


def swap(array, axis, bits):
    count = lax.axis_size(axis)
    return lax.ppermute(array, axis, [(i, i ^ bits) for i in range(count)])


def exchange(pieces):
    far = {bits: swap(pieces[bits], "ctx", bits) for bits in (1, 2, 3)}
    return [pieces[0]] + [far[bits] for bits in (1, 2, 3)]


def everyone(array, axis):
    return [array] + [swap(array, axis, bits) for bits in (1, 2, 3)]


def after(arrays, *others):
    return lax.optimization_barrier((arrays, others))[0]


def meet(kept, got):
    got = got.astype(F32)
    return (kept[1] + got[1]).astype(BF16), kept[0] + got[0]


def body(
    hidden, queries, keys, targets, lengths, value_matrix, attacker_down_factor, attacker_up_factor
):
    n_ctx, n_dp = lax.axis_size("ctx"), lax.axis_size("dp")
    rows, width = hidden.shape[2:]
    seq = rows * n_ctx
    value_span = value_matrix.shape[1]
    rank = attacker_up_factor.shape[0]
    factor = float(n_dp * seq) ** (-0.5)
    own = value_span // n_ctx
    ctx, dp = lax.axis_index("ctx"), lax.axis_index("dp")
    at = jnp.stack([ctx, dp]).astype(jnp.int32)
    h = hidden[0, 0]
    up = lax.dynamic_slice_in_dim(attacker_up_factor, ctx * own, own, axis=1)

    def block_of(array, parts, axis, bits):
        size = array.shape[axis] // parts
        return lax.dynamic_slice_in_dim(array, (ctx ^ bits) * size, size, axis=axis)

    qk = exchange(pair_columns(at, queries[0, 0], keys[0, 0], n_ctx))
    h = after((h,), qk[1])[0]
    low = dot(attacker_down_factor, h, 0, 1).astype(BF16)
    values = (dot(value_matrix, h, 0, 1) + dot(attacker_up_factor, low, 0, 0)).astype(BF16)
    carried = [
        jnp.concatenate([block_of(values, n_ctx, 0, bits), low], axis=0) for bits in range(n_ctx)
    ]
    h, carried = lax.optimization_barrier((h, carried))
    carried = exchange(carried)
    h_cols = [block_of(h, n_ctx, 1, bits) for bits in range(n_ctx)]
    h_cols[1] = swap(h_cols[1], "ctx", 1)
    h_cols[2], h_cols[3] = after((h_cols[2], h_cols[3]), h_cols[1])
    h_cols[2] = swap(h_cols[2], "ctx", 2)
    h_cols[3] = swap(h_cols[3], "ctx", 3)

    g, z = gram(at, lengths[0, 0], qk, targets[0, 0])
    carried = after(carried, h_cols[1])
    first, later, up_grad, low = first_pass(at, g, z, carried, up, rows, factor)
    first = everyone(first, "ctx")
    later = everyone(later, "ctx")

    low_rank, h_cols = down_pass(at, first, h_cols, up_grad)
    low_rank = everyone(low_rank, "dp")
    halves = [main_pass(at, h_cols, after(first, low_rank[1]))]
    low_rank = after(low_rank, halves[0][0], *later)
    moved, up_grad = moved_pass(low_rank, h_cols)
    halves.append(main_pass(at, h_cols, after(later, moved)))
    moved = everyone(moved, "ctx")
    halves = [meet(kept, swap(send, "dp", 1)) for send, kept in halves]
    moved = after(moved, halves[0][0])
    stepped = step_pass(moved, low, g, up, up_grad, rank * (width + value_span), factor)
    stepped = everyone(stepped, "ctx")
    passed = [swap(leaving, "dp", 2) for leaving, staying in halves]
    stepped = after(stepped, passed[0], halves[1][0])
    keep, *sent, rows_of_up = late_pass(at, h_cols, stepped, rank, own)
    late = [keep] + [swap(part, "dp", bits) for bits, part in zip((1, 2, 3), sent)]
    mains = []
    for (leaving, staying), block in zip(halves, passed):
        main = (staying + block.astype(F32)).astype(BF16)
        mains.append((main, swap(main, "adv", 1)))
    late = pack_pass(after(late, mains[1][0]), rows_of_up)
    late = [late, swap(late, "adv", 1)]
    return last_pass(mains, late, own, rank, -1.0 / lax.axis_size("adv"))


def doc_ids(lengths, seq):
    ends = jnp.cumsum(lengths)
    position = jnp.arange(seq, dtype=jnp.int32)
    return jnp.sum((position[:, None] >= ends[None, :]).astype(jnp.int32), axis=1)


def widen(array):
    rows = array.shape[0]
    heads = array.shape[1] // HD
    spread_out = jnp.repeat(array.reshape(rows, heads, HD), GROUP, axis=1)
    return spread_out.reshape(rows, heads * GROUP * HD)


def weight_blocks(q_heads, k_heads, docs):
    seq = q_heads.shape[0]
    block = seq // 8
    scale = HD ** (-0.5)
    position = jnp.arange(seq, dtype=jnp.int32)
    blocks = []
    for index in range(8):
        start = index * block
        stop = start + block
        scores = (
            jnp.einsum(
                "qhd,khd->hqk",
                q_heads[start:stop],
                k_heads[:stop],
                preferred_element_type=jnp.float32,
            )
            * scale
        )
        visible = (docs[start:stop, None] == docs[None, :stop]) & (
            position[None, :stop] <= position[start:stop, None]
        )
        scores = jnp.where(visible[None], scores, -1e30)
        top = jnp.max(scores, axis=2, keepdims=True)
        expo = jnp.exp(scores - top)
        blocks.append((expo / jnp.sum(expo, axis=2, keepdims=True)).astype(jnp.bfloat16))
    return blocks


def value_pass(blocks, v_heads, y_heads, factor):
    seq = v_heads.shape[0]
    block = seq // 8
    total = jnp.zeros(v_heads.shape, jnp.float32)
    for index in range(8):
        probs = blocks[index]
        start = index * block
        stop = start + block
        attn = jnp.einsum("hqk,khd->qhd", probs, v_heads[:stop], preferred_element_type=jnp.float32)
        d_attn = (factor * (attn - y_heads[start:stop].astype(jnp.float32))).astype(jnp.bfloat16)
        total = total.at[:stop].add(
            jnp.einsum("hqk,qhd->khd", probs, d_attn, preferred_element_type=jnp.float32)
        )
    return total.astype(jnp.bfloat16)


def plain_body(
    hidden, queries, keys, targets, lengths, value_matrix, attacker_down_factor, attacker_up_factor
):
    token_rows = hidden.shape[2]
    value_span = value_matrix.shape[1]
    n_ctx = lax.axis_size("ctx")
    seq = token_rows * n_ctx
    factor = float(lax.axis_size("dp") * seq) ** (-0.5)
    hidden_state_rows = hidden[0, 0]
    q_seq, k_seq = (
        lax.all_to_all(queries[0, 0], "ctx", split_axis=1, concat_axis=0, tiled=True),
        lax.all_to_all(widen(keys[0, 0]), "ctx", split_axis=1, concat_axis=0, tiled=True),
    )
    local_heads = q_seq.shape[1] // HD
    q_heads = q_seq.reshape(seq, local_heads, HD)
    k_heads = k_seq.reshape(seq, local_heads, HD)
    docs = doc_ids(lengths[0, 0], seq)
    blocks = weight_blocks(q_heads, k_heads, docs)
    y_heads = targets[0, 0].reshape(seq, local_heads, HD)
    starting_value = jnp.dot(hidden_state_rows, value_matrix, preferred_element_type=jnp.float32)
    reduce_over_rows = (((0,), (0,)), ((), ()))

    def value_weight_gradient(down_factor, up_factor, sign):
        attacker_input = jnp.dot(
            hidden_state_rows, down_factor, preferred_element_type=jnp.float32
        ).astype(jnp.bfloat16)
        value_rows = (
            starting_value + jnp.dot(attacker_input, up_factor, preferred_element_type=jnp.float32)
        ).astype(jnp.bfloat16)
        v_seq = lax.all_to_all(widen(value_rows), "ctx", split_axis=1, concat_axis=0, tiled=True)
        head_grads = value_pass(blocks, v_seq.reshape(seq, local_heads, HD), y_heads, sign * factor)
        back = lax.all_to_all(
            head_grads.reshape(seq, local_heads * HD),
            "ctx",
            split_axis=0,
            concat_axis=1,
            tiled=True,
        )
        grouped_rows = (
            back.reshape(token_rows, value_span // HD, GROUP, HD).astype(jnp.float32).sum(axis=2)
        )
        return (attacker_input, grouped_rows.reshape(token_rows, value_span).astype(jnp.bfloat16))

    attacker_input, leading_gradient = value_weight_gradient(
        attacker_down_factor, attacker_up_factor, 1.0
    )
    blended_output = lax.dot_general(
        leading_gradient,
        attacker_up_factor,
        (((1,), (1,)), ((), ())),
        preferred_element_type=jnp.float32,
    ).astype(jnp.bfloat16)
    down_gradient = lax.dot_general(
        hidden_state_rows, blended_output, reduce_over_rows, preferred_element_type=jnp.float32
    )
    up_gradient = lax.dot_general(
        attacker_input, leading_gradient, reduce_over_rows, preferred_element_type=jnp.float32
    )
    down_gradient, up_gradient = lax.psum((down_gradient, up_gradient), ("ctx", "dp"))
    count = down_gradient.size + up_gradient.size
    broadcast_rows = jnp.sqrt(
        (jnp.sum(down_gradient * down_gradient) + jnp.sum(up_gradient * up_gradient)) / count
        + 1e-06
    )
    stepped_down_factor = (
        attacker_down_factor.astype(jnp.float32) - ATTACK_STEP * down_gradient / broadcast_rows
    ).astype(jnp.bfloat16)
    stepped_up_factor = (
        attacker_up_factor.astype(jnp.float32) - ATTACK_STEP * up_gradient / broadcast_rows
    ).astype(jnp.bfloat16)
    unused, tamper = value_weight_gradient(stepped_down_factor, stepped_up_factor, -1.0)
    n_dp = lax.axis_size("dp")
    hidden_seq = lax.all_to_all(hidden_state_rows, "ctx", split_axis=1, concat_axis=0, tiled=True)
    hidden_all = lax.all_gather(hidden_seq, "dp", axis=0, tiled=True)
    grad_part = lax.all_to_all(tamper, "dp", split_axis=1, concat_axis=0, tiled=True)
    grad_all = lax.all_gather(grad_part, "ctx", axis=0, tiled=True)
    left = hidden_all.reshape(n_dp, n_ctx, token_rows, hidden_all.shape[1])
    right = grad_all.reshape(n_ctx, n_dp, token_rows, grad_all.shape[1])
    shares = jnp.einsum("dctx,cdty->xy", left, right, preferred_element_type=jnp.float32)
    total = lax.psum(shares, "adv")
    return total / lax.axis_size("adv")


def solution(mesh):
    sizes = mesh.shape
    fits = (sizes["ctx"], sizes["dp"], sizes["adv"]) == (4, 4, 2)
    placed = (
        P("adv", "dp", "ctx", None),
        P("adv", "dp", "ctx", None),
        P("adv", "dp", "ctx", None),
        P("adv", "dp", None, "ctx"),
        P("adv", "dp", None),
        P(),
        P(),
        P(),
    )
    return jax.shard_map(
        body if fits else plain_body,
        mesh=mesh,
        in_specs=placed,
        out_specs=P("ctx", "dp"),
        check_vma=False,
    )
```
